256 devices in a mesh: seq: 64 (over z, y, core), tensor: 4 (over x).
Axes of the slice: x: 4, y: 4, z: 8, core: 2. Of those that a mesh axis runs over, the one named last changes fastest.
Arguments:
- tokens: bfloat16 [8192, 1536], P('seq', 'tensor'), may hold values from -6 to 6
- attn_gain: float32 [1536], replicated, may hold values from 0.5 to 1.5
- q_weight: bfloat16 [1536, 1536], P(None, 'tensor'), may hold values from -0.15625 to 0.15625
- key_matrix: bfloat16 [1536, 512], P(None, 'tensor'), may hold values from -0.15625 to 0.15625
- value_matrix: bfloat16 [1536, 512], P(None, 'tensor'), may hold values from -0.15625 to 0.15625
- o_weight: bfloat16 [1536, 1536], P('tensor'), may hold values from -0.625 to 0.625
- moe_gain: float32 [1536], replicated, may hold values from 0.5 to 1.5
- gate_weight: bfloat16 [64, 1536, 512], P('seq', None, 'tensor'), may hold values from -0.15625 to 0.15625
- up_weight: bfloat16 [64, 1536, 512], P('seq', None, 'tensor'), may hold values from -0.15625 to 0.15625
- down_weight: bfloat16 [64, 512, 1536], P('seq', 'tensor'), may hold values from -0.25 to 0.25
- key_page_pool: bfloat16 [4096, 128, 512], P('seq', None, 'tensor'), may hold values from -140 to 140
- value_page_pool: bfloat16 [4096, 128, 512], P('seq', None, 'tensor'), may hold values from -6 to 6
- cache_lens: int32 [64], P('seq'), may hold values from 1 to 8192, as said below
- page_table: int32 [64, 64], P('seq'), may hold values from 0 to 63, each once within a row
- routes: int32 [8192, 8], P('seq'), may hold values from 0 to 39, all different within a row; in each aligned block of 128 rows (0 to 127, 128 to 255, ...) at most 32 rows name the same one
- route_gates: float32 [8192, 8], P('seq'), may hold values from 0.1 to 1
Outputs:
- mixed: bfloat16 [8192, 1536], P('seq', 'tensor')
The draws below stay inside these ranges and needn't reach their ends.
Inputs may be any that keep to these rules, and one draw needn't show every extreme that they name: `cache_lens`: some request has exactly 8192 cached tokens in every draw. `page_table`: each row is a permutation of 0 .. 63. `routes`: each row names 8 different experts. Among the 128 rows of one request no expert is named more than 32 times, a bound that some block reaches.
All inputs are finite; a program needn't handle non-finite values.
Results may differ from the reference program's by a relative error of at most 0.017.
The reference program's roundings to bfloat16 on the way count: a program that leaves them out, or rounds other values in their place, can miss the bound.
Values may be sent and summed in bfloat16 or wider, within the bound.
A program may use at most 128 MiB of HBM per device.

```python
import math
import jax
import jax.numpy as jnp
import numpy as np
from jax import lax

MODEL_WIDTH = 1536
QUERY_HEADS = 24
KEY_VALUE_HEADS = 8
HEAD_SIZE = 64
EXPERTS = 40
TOPK = 8
FFE = 512
PAGE_ROWS = 128
NEW_TOKENS = 128
LONGEST_LENGTH = 8192
CAP = 32
EXPERT_ROWS = 64
REQUEST_PAGES = 64
REQUEST_COUNT = 64
TOKENS = 8192
N_SEQ = 64


def draw_key_page_pool(key, part):
    draw_shape = (REQUEST_COUNT * REQUEST_PAGES, PAGE_ROWS, KEY_VALUE_HEADS * HEAD_SIZE)
    key_one = jax.random.fold_in(key, 0)
    return jnp.clip(2.0 * jax.random.normal(key_one, draw_shape, jnp.float32), -8.0, 8.0).astype(jnp.bfloat16)


def draw_cache_lens(key, part):
    key_one, key_two, key_three = jax.random.split(key, 3)
    factor_one = jax.random.randint(key_one, (REQUEST_COUNT,), 1, LONGEST_LENGTH + 1)
    factor_two = jax.random.randint(key_two, (REQUEST_COUNT,), 1, LONGEST_LENGTH + 1)
    lengths = jnp.maximum(factor_one * factor_two // LONGEST_LENGTH, 1)
    longest = jax.random.randint(key_three, (), 0, REQUEST_COUNT)
    return lengths.at[longest].set(LONGEST_LENGTH).astype(jnp.int32)


def level_of(stream_key, shape, shards, least, largest):
    loudness, own = 1.0, jax.random.fold_in(stream_key, 6)
    for position, parts in shards:
        heights = jnp.exp(jax.random.uniform(jax.random.fold_in(own, position), (parts,), jnp.float32, least / len(shards), largest / len(shards)))
        loudness = loudness * jnp.repeat(heights, shape[position] // parts).reshape([-1 if axis == position else 1 for axis in range(len(shape))])
    return loudness


def shared_out(key, own, number, rows, count, top, reach, lean):
    sequence = jax.random.permutation(key, count)
    crowded, ordinary = load_shares(count, rows * top, reach, lean, True), load_shares(count, rows * top, reach, lean, False)
    places = jnp.arange(count)

    def named(tallies, rotation):
        used = int((tallies > 0).sum())
        fixed = max(1, used // 4)
        moved = fixed + (places - fixed + rotation * (used - fixed)) % max(1, count - fixed)
        return jnp.zeros((count,), jnp.int32).at[sequence[jnp.where(places < fixed, places, moved)]].set(jnp.asarray(tallies, jnp.int32))

    tallies = jnp.where(number % 4 == 0, named(crowded, number // 4), named(ordinary, number - number // 4 - 1))
    mixed = jax.random.permutation(jax.random.fold_in(own, 3), count)
    giver, taker = mixed[0:count // 2 * 2:2], mixed[1:count // 2 * 2:2]
    room = jnp.minimum(tallies[giver] - 1, reach - tallies[taker]) // 2
    room = jnp.where((giver == sequence[0]) | (taker == sequence[0]) | (tallies[taker] == 0), 0, jnp.maximum(room, 0))
    moved = jax.random.randint(jax.random.fold_in(own, 4), (count // 2,), 0, 1 << 20) % (room + 1)
    tallies = tallies.at[giver].add(-moved).at[taker].add(moved)
    members = jnp.searchsorted(jnp.cumsum(tallies), jnp.arange(rows * top), side="right").astype(jnp.int32)
    listing = members.reshape(top, rows).T
    listing = listing[jax.random.permutation(jax.random.fold_in(own, 1), rows)]
    rotation = jax.random.randint(jax.random.fold_in(own, 2), (rows, 1), 0, top)
    return jnp.take_along_axis(listing, (jnp.arange(top)[None, :] + rotation) % top, axis=1)


def load_shares(number_of, total, reach, lean, full):
    loads = [(1 << 20) // math.isqrt(standing ** lean) + 1 for standing in range(1, number_of + 1)]
    largest = reach if full else min(reach, max(-(-total // number_of), total * loads[0] // sum(loads)))
    least = 1 if total - largest >= number_of - 1 else 0
    holding, rest = [largest] + [least] * (number_of - 1), total - largest - least * (number_of - 1)
    while rest > 0:
        movable = [i for i in range(1, number_of) if holding[i] < largest] or [i for i in range(1, number_of) if holding[i] < reach]
        mass, remaining = sum([loads[i] for i in movable]), rest
        for i in movable:
            more = min(reach - holding[i], max(1, remaining * loads[i] // mass), rest)
            holding[i] = holding[i] + more
            rest = rest - more
    return np.array(holding)


def centred(own_key, extent, width, limit, pieces=(), held_as=jnp.bfloat16):
    factor_of = level_of(own_key, extent, pieces, -0.22, 0.18) if pieces else 1.0
    values = jax.random.normal(own_key, extent, jnp.float32) * width * factor_of
    return jnp.minimum(jnp.maximum(values, -limit), limit).astype(held_as)


def setup_inputs(seed: int = 0) -> dict:
    key_list = jax.random.split(jax.random.key(seed), 17)
    tokens = centred(key_list[0], (TOKENS, MODEL_WIDTH), 1.0, 6.0, ((0, 64), (1, 4)))
    attn_gain = jnp.clip(1.0 + 0.1 * jax.random.normal(key_list[1], (MODEL_WIDTH,), jnp.float32), 0.5, 1.5)
    q_weight = centred(key_list[2], (MODEL_WIDTH, QUERY_HEADS * HEAD_SIZE), MODEL_WIDTH ** -0.5, 0.15625, ((1, 4),))
    key_matrix = centred(key_list[3], (MODEL_WIDTH, KEY_VALUE_HEADS * HEAD_SIZE), MODEL_WIDTH ** -0.5, 0.15625, ((1, 4),))
    value_matrix = centred(key_list[4], (MODEL_WIDTH, KEY_VALUE_HEADS * HEAD_SIZE), MODEL_WIDTH ** -0.5, 0.15625, ((1, 4),))
    o_weight = centred(key_list[5], (QUERY_HEADS * HEAD_SIZE, MODEL_WIDTH), (QUERY_HEADS * HEAD_SIZE // 16) ** -0.5, 0.625, ((0, 4),))
    moe_gain = jnp.clip(1.0 + 0.1 * jax.random.normal(key_list[6], (MODEL_WIDTH,), jnp.float32), 0.5, 1.5)
    gate_weight = centred(key_list[7], (EXPERT_ROWS, MODEL_WIDTH, FFE), MODEL_WIDTH ** -0.5, 0.15625, ((0, 64), (2, 4)))
    up_weight = centred(key_list[8], (EXPERT_ROWS, MODEL_WIDTH, FFE), MODEL_WIDTH ** -0.5, 0.15625, ((0, 64), (2, 4)))
    down_weight = centred(key_list[9], (EXPERT_ROWS, FFE, MODEL_WIDTH), FFE ** -0.5, 0.25, ((0, 64), (1, 4)))
    key_page_pool = draw_key_page_pool(jax.random.fold_in(key_list[16], 71), 0)
    value_page_pool = centred(key_list[11], (REQUEST_COUNT * REQUEST_PAGES, PAGE_ROWS, KEY_VALUE_HEADS * HEAD_SIZE), 1.0, 6.0, ((0, 64), (2, 4)))
    cache_lens = draw_cache_lens(jax.random.fold_in(key_list[16], 71), 0)
    page_table = jax.vmap(lambda own: jax.random.permutation(own, REQUEST_PAGES))(jax.random.split(key_list[13], REQUEST_COUNT)).reshape((REQUEST_COUNT, REQUEST_PAGES)).astype(jnp.int32)
    routes_keys = jax.random.split(jax.random.fold_in(key_list[14], 1), TOKENS // NEW_TOKENS)
    routes_turns = jax.random.permutation(jax.random.fold_in(key_list[14], 3), TOKENS // NEW_TOKENS)
    routes = jax.vmap(lambda own, number: shared_out(jax.random.fold_in(key_list[14], 2), own, number, NEW_TOKENS, EXPERTS, TOPK, CAP, 1))(routes_keys, routes_turns).reshape((TOKENS, TOPK))
    route_gates = jnp.clip(jnp.exp(math.log(1.0) - 2.3025851 * jax.random.uniform(key_list[15], (TOKENS, TOPK), jnp.float32) ** level_of(key_list[15], (TOKENS, TOPK), ((0, 64),), -0.2, 0.2)), 0.1, 1.0)
    return dict(tokens=tokens, attn_gain=attn_gain, q_weight=q_weight, key_matrix=key_matrix, value_matrix=value_matrix, o_weight=o_weight, moe_gain=moe_gain, gate_weight=gate_weight, up_weight=up_weight, down_weight=down_weight, key_page_pool=key_page_pool, value_page_pool=value_page_pool, cache_lens=cache_lens, page_table=page_table, routes=routes, route_gates=route_gates)


NORM_EPSILON = 1e-06
MASKED_SCORE = -1e+30

def norm_rows(field, gain_row):
    widened = field.astype(jnp.float32)
    return widened * lax.rsqrt(lax.optimization_barrier(jnp.mean(widened * widened, axis=1, keepdims=True)) + NORM_EPSILON) * gain_row

def apply_rotary(field, token_places):
    head_dim = field.shape[-1]
    half_dim = head_dim // 2
    frequency = 10000.0 ** (-2.0 * jnp.arange(half_dim, dtype=jnp.float32) / head_dim)
    phase_angle = token_places[:, None, None] * frequency
    cosine = jnp.cos(phase_angle)
    sine_part = jnp.sin(phase_angle)
    lower_half = field[..., :half_dim]
    upper_half = field[..., half_dim:]
    return jnp.concatenate([lower_half * cosine - upper_half * sine_part, upper_half * cosine + lower_half * sine_part], axis=-1)

def page_rounded_length(field):
    return lax.optimization_barrier(field.astype(jnp.bfloat16)).astype(jnp.float32)

def reference(tokens, attn_gain, q_weight, key_matrix, value_matrix, o_weight, moe_gain, gate_weight, up_weight, down_weight, key_page_pool, value_page_pool, cache_lens, page_table, routes, route_gates):
    normed = norm_rows(tokens, attn_gain).astype(jnp.bfloat16)
    queries_all = jnp.dot(normed, q_weight, preferred_element_type=jnp.float32)
    joined_keys = jnp.dot(normed, key_matrix, preferred_element_type=jnp.float32)
    joined_values = jnp.dot(normed, value_matrix, preferred_element_type=jnp.float32)
    query_group_width = QUERY_HEADS // KEY_VALUE_HEADS
    score_scale = HEAD_SIZE ** (-0.5)

    def one_request(request):
        first_row_index = request * NEW_TOKENS
        token_places = (cache_lens[request] + jnp.arange(NEW_TOKENS, dtype=jnp.int32)).astype(jnp.float32)
        query_rows = lax.dynamic_slice_in_dim(queries_all, first_row_index, NEW_TOKENS, 0).reshape(NEW_TOKENS, QUERY_HEADS, HEAD_SIZE)
        query_rows = page_rounded_length(apply_rotary(query_rows, token_places)).reshape(NEW_TOKENS, KEY_VALUE_HEADS, query_group_width, HEAD_SIZE)
        incoming_keys = lax.dynamic_slice_in_dim(joined_keys, first_row_index, NEW_TOKENS, 0).reshape(NEW_TOKENS, KEY_VALUE_HEADS, HEAD_SIZE)
        incoming_keys = page_rounded_length(apply_rotary(incoming_keys, token_places))
        incoming_values = page_rounded_length(lax.dynamic_slice_in_dim(joined_values, first_row_index, NEW_TOKENS, 0).reshape(NEW_TOKENS, KEY_VALUE_HEADS, HEAD_SIZE))
        occupied_pages = request * REQUEST_PAGES + page_table[request]
        stored_keys = key_page_pool[occupied_pages].reshape(LONGEST_LENGTH, KEY_VALUE_HEADS, HEAD_SIZE).astype(jnp.float32)
        stored_values = value_page_pool[occupied_pages].reshape(LONGEST_LENGTH, KEY_VALUE_HEADS, HEAD_SIZE).astype(jnp.float32)
        cache_scores = jnp.einsum('tgjd,sgd->gjts', query_rows, stored_keys) * score_scale
        cache_scores = jnp.where(jnp.arange(LONGEST_LENGTH, dtype=jnp.int32) < cache_lens[request], cache_scores, MASKED_SCORE)
        fresh_scores = jnp.einsum('tgjd,sgd->gjts', query_rows, incoming_keys) * score_scale
        causal = jnp.arange(NEW_TOKENS)[None, :] <= jnp.arange(NEW_TOKENS)[:, None]
        fresh_scores = jnp.where(causal, fresh_scores, MASKED_SCORE)
        row_best = jnp.maximum(lax.optimization_barrier(jnp.max(cache_scores, axis=-1)), lax.optimization_barrier(jnp.max(fresh_scores, axis=-1)))
        cache_weights = jnp.exp(cache_scores - row_best[..., None])
        fresh_weights = jnp.exp(fresh_scores - row_best[..., None])
        denominator = lax.optimization_barrier(jnp.sum(cache_weights, axis=-1)) + lax.optimization_barrier(jnp.sum(fresh_weights, axis=-1))
        mixture = jnp.einsum('gjts,sgd->gjtd', page_rounded_length(cache_weights), stored_values)
        mixture = mixture + jnp.einsum('gjts,sgd->gjtd', page_rounded_length(fresh_weights), incoming_values)
        result = mixture / denominator[..., None]
        return jnp.transpose(result, (2, 0, 1, 3)).reshape(NEW_TOKENS, QUERY_HEADS * HEAD_SIZE).astype(jnp.bfloat16)
    attended = lax.map(one_request, jnp.arange(REQUEST_COUNT, dtype=jnp.int32)).reshape(TOKENS, QUERY_HEADS * HEAD_SIZE)
    partial_value = jnp.dot(attended, o_weight, preferred_element_type=jnp.float32)
    residual = (tokens.astype(jnp.float32) + partial_value).astype(jnp.bfloat16)
    moe_in = norm_rows(residual, moe_gain).astype(jnp.bfloat16)
    expert_of = routes.reshape(-1)
    token_of = jnp.arange(TOKENS * TOPK, dtype=jnp.int32) // TOPK
    gate_of = route_gates.reshape(-1)
    slot_bound = N_SEQ * CAP
    row_block = min(256, slot_bound)

    def one_expert(carried_sum, expert):
        chosen = expert_of == expert
        row_total = jnp.sum(chosen.astype(jnp.int32))
        picked_rows = jnp.nonzero(chosen, size=slot_bound, fill_value=0)[0].astype(jnp.int32)

        def one_block(block_id, running):
            block_rows = lax.dynamic_slice_in_dim(picked_rows, block_id * row_block, row_block)
            live_rows = block_id * row_block + jnp.arange(row_block, dtype=jnp.int32) < row_total
            token_rows = token_of[block_rows]
            inputs = moe_in[token_rows]
            gate_act = jnp.dot(inputs, gate_weight[expert], preferred_element_type=jnp.float32)
            up_act = jnp.dot(inputs, up_weight[expert], preferred_element_type=jnp.float32)
            hidden = (jax.nn.silu(gate_act) * up_act).astype(jnp.bfloat16)
            output = page_rounded_length(jnp.dot(hidden, down_weight[expert], preferred_element_type=jnp.float32))
            weight = jnp.where(live_rows, gate_of[block_rows], 0.0)
            return running.at[token_rows].add(output * weight[:, None])
        block_total = (row_total + row_block - 1) // row_block
        return (lax.fori_loop(0, block_total, one_block, carried_sum), None)
    expert_mix, _ = lax.scan(one_expert, jnp.zeros((TOKENS, MODEL_WIDTH), jnp.float32), jnp.arange(EXPERTS, dtype=jnp.int32))
    return (residual.astype(jnp.float32) + expert_mix).astype(jnp.bfloat16)
```

```python
import jax
import jax.numpy as jnp
from jax import lax
from jax.experimental import pallas as pl
from jax.experimental.pallas import tpu as pltpu
from jax.sharding import PartitionSpec as P

MESH = pl.DeviceIdType.MESH
BF16 = jnp.bfloat16
F32 = jnp.float32
HEAD = 64
NORM_EPSILON = 1e-06
MASKED_SCORE = -1e30
NX, NY, NZ = 4, 4, 8
ROWS = 128
QUARTER = ROWS // NX
HALF = QUARTER // 2
WIDTH = 1536
COLS = WIDTH // NX
AUG = WIDTH + 128
HEADS = 6
STACK = HEADS * ROWS
CACHE = 8192
BLOCK = 1024
BLOCKS = CACHE // BLOCK
PAGE = 128
FFE = 512


def whereabouts():
    seq = lax.axis_index("seq")
    x = lax.axis_index("tensor")
    core = lax.rem(seq, 2)
    y = lax.rem(lax.div(seq, 2), NY)
    z = lax.div(seq, 2 * NY)
    return x, y, z, core


def device(x, y, z, core):
    return ((z * NY + y) * 2 + core, x)


def send_to(src, dst, send_sem, recv_sem, target):
    return pltpu.make_async_remote_copy(
        src_ref=src,
        dst_ref=dst,
        send_sem=send_sem,
        recv_sem=recv_sem,
        device_id=target,
        device_id_type=MESH,
    )


def greet(targets):
    barrier = pltpu.get_barrier_semaphore()
    for target in targets:
        pl.semaphore_signal(barrier, inc=1, device_id=target, device_id_type=MESH)
    pl.semaphore_wait(barrier, len(targets))


def norm_rows(widened, gain_row):
    return (
        widened
        * lax.rsqrt(jnp.mean(widened * widened, axis=1, keepdims=True) + NORM_EPSILON)
        * gain_row
    )


def swap_halves(block):
    lane = lax.broadcasted_iota(jnp.int32, block.shape, 1)
    return jnp.where(
        lax.rem(lane, HEAD) < HEAD // 2,
        pltpu.roll(block, 128 - HEAD // 2, 1),
        pltpu.roll(block, HEAD // 2, 1),
    )


def attend_kernel(
    seen_ref,
    tokens_ref,
    cos_ref,
    sin_ref,
    routes_ref,
    gates_ref,
    attn_gain_ref,
    moe_gain_ref,
    q_hbm,
    k_hbm,
    v_hbm,
    o_hbm,
    key_pool,
    value_pool,
    gate_hbm,
    up_hbm,
    down_hbm,
    aug_ref,
    resid_ref,
    gate_all,
    up_all,
    down_all,
    tok,
    qw,
    kw,
    vw,
    ow,
    keys,
    values,
    stacked,
    best,
    total,
    mix,
    stage,
    arrived,
    partial,
    load_sem,
    key_sem,
    value_sem,
    tok_send,
    tok_recv,
    sum_send,
    sum_recv,
    w_send,
    w_recv,
):
    x, y, z, core = whereabouts()
    peers = [lax.rem(x + j, NX) for j in range(NX)]
    loads = []
    for number, (src, dst) in enumerate(
        ((q_hbm, qw), (k_hbm, kw), (v_hbm, vw), (o_hbm, ow))
    ):
        copy = pltpu.make_async_copy(src, dst, load_sem.at[number])
        copy.start()
        loads.append(copy)

    def key_copy(i):
        rows = pl.ds(pl.multiple_of(i * BLOCK, BLOCK), BLOCK)
        return pltpu.make_async_copy(
            key_pool.at[rows, :], keys.at[rows, pl.ds(0, 128)], key_sem.at[i]
        )

    def value_copy(i):
        rows = pl.ds(pl.multiple_of(i * BLOCK, BLOCK), BLOCK)
        return pltpu.make_async_copy(
            value_pool.at[rows, :], values.at[rows, :], value_sem.at[i]
        )

    for i in range(BLOCKS):
        key_copy(i).start()
        value_copy(i).start()

    greet([device(peers[j], y, z, core) for j in range(1, NX)])
    sends = []
    for j in range(1, NX):
        copy = send_to(
            tokens_ref,
            tok.at[x],
            tok_send.at[j],
            tok_recv.at[j],
            device(peers[j], y, z, core),
        )
        copy.start()
        sends.append(copy)
    tok[x] = tokens_ref[...]
    weight_waits = []
    for number, (src, dst) in enumerate(
        ((gate_hbm, gate_all), (up_hbm, up_all), (down_hbm, down_all))
    ):
        for way, j in enumerate((1, NX - 1)):
            copy = send_to(
                src,
                dst.at[x],
                w_send.at[2 * number + way],
                w_recv.at[2 * number + way],
                device(peers[j], y, z, core),
            )
            copy.start()
            sends.append(copy)
            weight_waits.append(
                send_to(
                    src,
                    dst.at[peers[NX - j]],
                    w_send.at[2 * number + way],
                    w_recv.at[2 * number + way],
                    device(peers[j], y, z, core),
                )
            )

    row = lax.broadcasted_iota(jnp.int32, (PAGE, 128), 0)
    lane = lax.broadcasted_iota(jnp.int32, (PAGE, 128), 1)

    def write_bias(p, carry):
        hidden_row = (lane == 0) & (row >= seen_ref[p])
        keys[pl.ds(pl.multiple_of(p * PAGE, PAGE), PAGE), pl.ds(128, 128)] = jnp.where(
            hidden_row, MASKED_SCORE, 0.0
        ).astype(BF16)
        return carry

    lax.fori_loop(0, CACHE // PAGE, write_bias, 0)

    for j in range(1, NX):
        send_to(
            tokens_ref,
            tok.at[peers[NX - j]],
            tok_send.at[j],
            tok_recv.at[j],
            device(peers[j], y, z, core),
        ).wait_recv()
    whole = jnp.concatenate([tok[j].astype(F32) for j in range(NX)], axis=1)
    normed = norm_rows(whole, attn_gain_ref[...]).astype(BF16)
    for copy in loads:
        copy.wait()
    cosine = cos_ref[...]
    sine = sin_ref[...]
    scale = HEAD ** (-0.5)
    queries = jnp.dot(normed, qw[...], preferred_element_type=F32)
    first_bias = jnp.where(lane == 0, 1.0, 0.0).astype(BF16)
    for pair in range(HEADS // 2):
        block = queries[:, pair * 128 : (pair + 1) * 128]
        turned = (block * cosine + swap_halves(block) * sine).astype(BF16)
        turned = turned.astype(F32) * scale
        crossed = pltpu.roll(turned, HEAD, 1)
        for side in range(2):
            head = 2 * pair + side
            group = head // 3
            placed = turned if side == group else crossed
            mine = (lane < HEAD) if group == 0 else (lane >= HEAD)
            stacked[pl.ds(head * ROWS, ROWS), pl.ds(0, 128)] = jnp.where(
                mine, placed, 0.0
            ).astype(BF16)
            stacked[pl.ds(head * ROWS, ROWS), pl.ds(128, 128)] = first_bias
    new_keys = jnp.dot(normed, kw[...], preferred_element_type=F32)
    new_keys = (new_keys * cosine + swap_halves(new_keys) * sine).astype(BF16)
    new_values = jnp.dot(normed, vw[...], preferred_element_type=F32).astype(BF16)

    scores = lax.dot_general(
        stacked[:, 0:128],
        new_keys,
        (((1,), (1,)), ((), ())),
        preferred_element_type=F32,
    )
    query_row = lax.rem(lax.broadcasted_iota(jnp.int32, (STACK, ROWS), 0), ROWS)
    key_row = lax.broadcasted_iota(jnp.int32, (STACK, ROWS), 1)
    scores = jnp.where(key_row <= query_row, scores, MASKED_SCORE)
    top = jnp.max(scores, axis=1, keepdims=True)
    weights = jnp.exp(scores - top)
    best[...] = top
    total[...] = jnp.sum(weights, axis=1, keepdims=True)
    mix[...] = jnp.dot(weights.astype(BF16), new_values, preferred_element_type=F32)

    def step(i, carry):
        key_copy(i).wait()
        value_copy(i).wait()
        rows = pl.ds(pl.multiple_of(i * BLOCK, BLOCK), BLOCK)
        scores = lax.dot_general(
            stacked[...],
            keys[rows, :],
            (((1,), (1,)), ((), ())),
            preferred_element_type=F32,
        )
        old = best[...]
        new = jnp.maximum(old, jnp.max(scores, axis=1, keepdims=True))
        shrink = jnp.exp(old - new)
        weights = jnp.exp(scores - new)
        best[...] = new
        total[...] = total[...] * shrink + jnp.sum(weights, axis=1, keepdims=True)
        mix[...] = mix[...] * shrink + jnp.dot(
            weights.astype(BF16), values[rows, :], preferred_element_type=F32
        )
        return carry

    lax.fori_loop(0, BLOCKS, step, 0)
    result = mix[...] / total[...]
    pieces = []
    for pair in range(HEADS // 2):
        sides = []
        for side in range(2):
            head = 2 * pair + side
            block = result[head * ROWS : (head + 1) * ROWS, :]
            sides.append(block if side == head // 3 else pltpu.roll(block, HEAD, 1))
        pieces.append(jnp.where(lane < HEAD, sides[0], sides[1]).astype(BF16))
    attended = jnp.concatenate(pieces, axis=1)
    summand = jnp.dot(attended, ow[...], preferred_element_type=F32)
    for j in range(NX):
        quarter = summand[j * QUARTER : (j + 1) * QUARTER, :]
        partial[j] = quarter
        stage[j] = quarter.astype(BF16)
    for j in range(1, NX):
        copy = send_to(
            stage.at[peers[j]],
            arrived.at[x],
            sum_send.at[j],
            sum_recv.at[j],
            device(peers[j], y, z, core),
        )
        copy.start()
        sends.append(copy)

    my_rows = pl.ds(pl.multiple_of(x * QUARTER, QUARTER), QUARTER)
    expert = lax.rem(lax.broadcasted_iota(jnp.int32, (QUARTER, 128), 1), 64)
    low = lax.broadcasted_iota(jnp.int32, (QUARTER, 128), 1) >= 64
    routes = routes_ref[my_rows, :]
    gates = gates_ref[my_rows, :]
    chosen = jnp.zeros((QUARTER, 128), F32)
    for k in range(routes.shape[1]):
        chosen = chosen + jnp.where(routes[:, k : k + 1] == expert, gates[:, k : k + 1], 0.0)
    high_part = chosen.astype(BF16).astype(F32)
    aug_ref[:, WIDTH:AUG] = jnp.where(low, chosen - high_part, high_part).astype(BF16)
    residual = partial[x] + jnp.concatenate(
        [tok[j, my_rows, :].astype(F32) for j in range(NX)], axis=1
    )
    for j in range(1, NX):
        send_to(
            stage.at[peers[j]],
            arrived.at[peers[NX - j]],
            sum_send.at[j],
            sum_recv.at[j],
            device(peers[j], y, z, core),
        ).wait_recv()
        residual = residual + arrived[peers[NX - j]].astype(F32)
    residual = residual.astype(BF16)
    resid_ref[...] = residual
    aug_ref[:, 0:WIDTH] = norm_rows(residual.astype(F32), moe_gain_ref[...]).astype(BF16)
    for copy in weight_waits:
        copy.wait_recv()
    for copy in sends:
        copy.wait_send()


class Gather:
    def __init__(self, size, me, target, place, halves, send_sem, recv_sem):
        self.size, self.me, self.target = size, me, target
        self.place, self.halves = place, halves
        self.send_sem, self.recv_sem = send_sem, recv_sem
        self.sent = []

    def copies(self, k, arriving):
        last = k + 1 == self.size // 2
        made = []
        for way in range(2):
            if arriving:
                shift = -(1 + k) if way == 0 else 1 + k
            else:
                shift = -k if way == 0 else k
            ref = self.place(lax.rem(self.me + shift + self.size, self.size))
            if last:
                ref = self.halves(ref)[way]
            made.append(
                send_to(
                    ref,
                    ref,
                    self.send_sem.at[way, k],
                    self.recv_sem.at[way, k],
                    self.target(1 if way == 0 else -1),
                )
            )
        return made

    def send(self, k):
        for copy in self.copies(k, False):
            copy.start()
            self.sent.append(copy)

    def wait(self, k):
        for copy in self.copies(k, True):
            copy.wait_recv()


class Scatter:
    def __init__(self, size, me, target, own, halves, stage, arrived, send_sem, recv_sem):
        self.size, self.me, self.target = size, me, target
        self.own, self.halves = own, halves
        self.stage, self.arrived = stage, arrived
        self.send_sem, self.recv_sem = send_sem, recv_sem
        self.sent = []

    def copy(self, way, k):
        src, dst = self.stage.at[way, k], self.arrived.at[way, k]
        if k == 0:
            src, dst = self.halves(src)[way], self.halves(dst)[way]
        return send_to(
            src,
            dst,
            self.send_sem.at[way, k],
            self.recv_sem.at[way, k],
            self.target(1 if way == 0 else -1),
        )

    def send(self, k):
        distance = self.size // 2 - k
        for way in range(2):
            shift = distance if way == 0 else -distance
            own = self.own(lax.rem(self.me + shift + self.size, self.size))
            here = self.stage.at[way, k]
            if k == 0:
                self.halves(here)[way][...] = self.halves(own)[way][...].astype(BF16)
            elif k == 1:
                self.copy(way, 0).wait_recv()
                came = self.halves(self.arrived.at[way, 0])[way]
                self.halves(here)[way][...] = (
                    self.halves(own)[way][...] + came[...].astype(F32)
                ).astype(BF16)
                self.halves(here)[1 - way][...] = self.halves(own)[1 - way][...].astype(BF16)
            else:
                self.copy(way, k - 1).wait_recv()
                here[...] = (own[...] + self.arrived[way, k - 1].astype(F32)).astype(BF16)
            copy = self.copy(way, k)
            copy.start()
            self.sent.append(copy)

    def result(self):
        k = self.size // 2 - 1
        answer = self.own(self.me)[...]
        for way in range(2):
            self.copy(way, k).wait_recv()
            answer = answer + self.arrived[way, k].astype(F32)
        return answer


def half_columns(ref):
    width = ref.shape[-1]
    split = (width // 256 + (width // 128) % 2) * 128
    lead = (slice(None),) * (len(ref.shape) - 1)
    return (
        ref.at[(*lead, pl.ds(0, split))],
        ref.at[(*lead, pl.ds(split, width - split))],
    )


def half_rows(ref):
    size = ref.shape[0] // 2
    return ref.at[pl.ds(0, size)], ref.at[pl.ds(size, size)]


def expert_kernel(
    aug_hbm,
    resid_ref,
    gate_hbm,
    up_hbm,
    down_hbm,
    gate_all,
    up_all,
    down_all,
    out_ref,
    rows_a,
    rows_b,
    wg,
    wu,
    wd,
    out_a,
    out_b,
    sum_a,
    sum_b,
    stage_az,
    came_az,
    stage_ay,
    came_ay,
    stage_by,
    came_by,
    stage_bz,
    came_bz,
    mixed,
    came_x,
    in_sem,
    near_sem,
    far_send,
    far_recv,
    part_send,
    part_recv,
    ay_send,
    ay_recv,
    az_send,
    az_recv,
    by_send,
    by_recv,
    bz_send,
    bz_recv,
    ry_send,
    ry_recv,
    raz_send,
    raz_recv,
    rby_send,
    rby_recv,
    rbz_send,
    rbz_recv,
    x_send,
    x_recv,
):
    x, y, z, core = whereabouts()
    x_peers = [lax.rem(x + j, NX) for j in range(NX)]
    y_peers = [lax.rem(y + j, NY) for j in range(NY)]
    z_at = lambda step: lax.rem(z + step + NZ, NZ)
    partner = device(x, y, z, 1 - core)
    greet(
        [device(x_peers[j], y, z, core) for j in range(1, NX)]
        + [device(x, y_peers[j], z, core) for j in range(1, NY)]
        + [device(x, y, z_at(1), core), device(x, y, z_at(-1), core), partner]
    )
    into_a = pltpu.make_async_copy(aug_hbm.at[pl.ds(0, HALF)], rows_a.at[z, y], in_sem.at[0])
    into_b = pltpu.make_async_copy(aug_hbm.at[pl.ds(HALF, HALF)], rows_b.at[y, z], in_sem.at[1])
    into_a.start()
    into_b.start()
    sent = []

    def columns(w, q):
        return w.at[core, :, pl.ds(pl.multiple_of(q * 128, 128), 128)]

    def depth(w, q):
        return w.at[core, pl.ds(pl.multiple_of(q * 128, 128), 128), :]

    into_a.wait()
    into_b.wait()

    for j in range(1, NY):
        copy = send_to(
            rows_a.at[z, y],
            rows_a.at[z, y],
            ay_send.at[j],
            ay_recv.at[j],
            device(x, y_peers[j], z, core),
        )
        copy.start()
        sent.append(copy)
    to_z = lambda step: device(x, y, z_at(step), core)
    to_y = lambda step: device(x, y_peers[step % NY], z, core)
    gather_az = Gather(NZ, z, to_z, lambda i: rows_a.at[i], half_rows, az_send, az_recv)
    gather_bz = Gather(NZ, z, to_z, lambda i: rows_b.at[y, i], half_columns, bz_send, bz_recv)
    gather_by = Gather(NY, y, to_y, lambda i: rows_b.at[i], half_rows, by_send, by_recv)
    gather_bz.send(0)

    far = lax.rem(x + 2, NX)
    for number, (src, dst) in enumerate(((gate_all, wg), (up_all, wu), (down_all, wd))):
        size = src.shape[1] // 2
        for way, j in enumerate((1, NX - 1)):
            q = x_peers[NX - j]
            rows = pl.ds(way * size, size)
            if number < 2:
                place = dst.at[core, rows, pl.ds(pl.multiple_of(q * 128, 128), 128)]
            else:
                place = dst.at[core, pl.ds(pl.multiple_of(q * 128 + way * size, size), size), :]
            copy = send_to(
                src.at[q, rows, :],
                place,
                far_send.at[number, way],
                far_recv.at[number, way],
                device(x_peers[j], y, z, core),
            )
            copy.start()
            sent.append(copy)
    near = []
    for number, (mine, others, dst, cut) in enumerate(
        (
            (gate_hbm, gate_all, wg, columns),
            (up_hbm, up_all, wu, columns),
            (down_hbm, down_all, wd, depth),
        )
    ):
        for which, j in enumerate((0, 1, NX - 1)):
            q = x_peers[j]
            src = mine if j == 0 else others.at[q]
            copy = pltpu.make_async_copy(src, cut(dst, q), near_sem.at[number, which])
            copy.start()
            near.append(copy)
            copy = send_to(
                src,
                cut(dst, q),
                part_send.at[number, which],
                part_recv.at[number, which],
                partner,
            )
            copy.start()
            sent.append(copy)

    for j in range(1, NY):
        place = rows_a.at[z, y_peers[NY - j]]
        send_to(
            place, place, ay_send.at[j], ay_recv.at[j], device(x, y_peers[j], z, core)
        ).wait_recv()
    gather_az.send(0)
    gather_bz.wait(0)
    gather_bz.send(1)
    gather_bz.wait(1)
    gather_bz.send(2)
    gather_az.wait(0)
    gather_az.send(1)
    gather_bz.wait(2)
    gather_bz.send(3)
    gather_bz.wait(3)
    gather_by.send(0)
    gather_az.wait(1)
    gather_az.send(2)
    gather_az.wait(2)
    gather_az.send(3)
    for number, (dst, cut) in enumerate(((wg, columns), (wu, columns), (wd, depth))):
        size = (WIDTH if number < 2 else 128) // 2
        for way, j in enumerate((1, NX - 1)):
            rows = pl.ds(way * size, size)
            if number < 2:
                place = dst.at[core, rows, pl.ds(pl.multiple_of(far * 128, 128), 128)]
            else:
                place = dst.at[core, pl.ds(pl.multiple_of(far * 128 + way * size, size), size), :]
            send_to(
                place,
                place,
                far_send.at[number, way],
                far_recv.at[number, way],
                device(x_peers[j], y, z, core),
            ).wait_recv()
        copy = send_to(
            cut(dst, far),
            cut(dst, far),
            part_send.at[number, 3],
            part_recv.at[number, 3],
            partner,
        )
        copy.start()
        sent.append(copy)
    gather_by.wait(0)
    gather_by.send(1)
    gather_az.wait(3)
    for copy in near:
        copy.wait()

    def partner_columns(w, q):
        return w.at[1 - core, :, pl.ds(pl.multiple_of(q * 128, 128), 128)]

    def partner_depth(w, q):
        return w.at[1 - core, pl.ds(pl.multiple_of(q * 128, 128), 128), :]

    for number, (dst, cut) in enumerate(
        ((wg, partner_columns), (wu, partner_columns), (wd, partner_depth))
    ):
        for which, j in enumerate((0, 1, NX - 1, 2)):
            place = cut(dst, x_peers[j])
            send_to(
                place,
                place,
                part_send.at[number, which],
                part_recv.at[number, which],
                partner,
            ).wait_recv()

    first_expert = 2 * (z * NY + y)

    def compute(rows, out, steps):
        lead = rows.shape[0] // steps
        count = lead * rows.shape[1] * rows.shape[2]

        def chunk(i, carry):
            part = pl.ds(i * lead, lead)
            block = rows[part].reshape(count, AUG)
            inputs = block[:, 0:WIDTH]
            gates = block[:, WIDTH:AUG].astype(F32)
            lane = lax.rem(lax.broadcasted_iota(jnp.int32, (count, 128), 1), 64)
            answer = None
            for e in range(2):
                gate = jnp.sum(
                    jnp.where(lane == first_expert + e, gates, 0.0), axis=1, keepdims=True
                )
                gate_act = jnp.dot(inputs, wg[e], preferred_element_type=F32)
                up_act = jnp.dot(inputs, wu[e], preferred_element_type=F32)
                hidden = (gate_act / (1.0 + jnp.exp(-gate_act)) * up_act * gate).astype(BF16)
                term = jnp.dot(hidden, wd[e], preferred_element_type=F32)
                answer = term if answer is None else answer + term
            out[part] = answer.reshape(lead, rows.shape[1], rows.shape[2], WIDTH)
            return carry

        lax.fori_loop(0, steps, chunk, 0)

    scatter_az = Scatter(
        NZ, z, to_z, lambda i: out_a.at[i], half_rows, stage_az, came_az, raz_send, raz_recv
    )
    scatter_by = Scatter(
        NY, y, to_y, lambda i: out_b.at[i], half_rows, stage_by, came_by, rby_send, rby_recv
    )
    scatter_bz = Scatter(
        NZ, z, to_z, lambda i: sum_b.at[i], half_columns, stage_bz, came_bz, rbz_send, rbz_recv
    )
    compute(rows_a, out_a, 2)
    scatter_az.send(0)
    gather_by.wait(1)
    compute(rows_b, out_b, 2)
    scatter_by.send(0)
    scatter_az.send(1)
    scatter_by.send(1)
    scatter_az.send(2)
    scatter_az.send(3)
    sum_b[...] = scatter_by.result()
    scatter_bz.send(0)
    sum_a[...] = scatter_az.result()
    stage_ay[...] = sum_a[...].astype(BF16)
    for j in range(1, NY):
        copy = send_to(
            stage_ay.at[y_peers[j]],
            came_ay.at[y],
            ry_send.at[j],
            ry_recv.at[j],
            device(x, y_peers[j], z, core),
        )
        copy.start()
        sent.append(copy)
    scatter_bz.send(1)
    scatter_bz.send(2)
    scatter_bz.send(3)
    upper = sum_a[y]
    for j in range(1, NY):
        send_to(
            stage_ay.at[y_peers[j]],
            came_ay.at[y_peers[NY - j]],
            ry_send.at[j],
            ry_recv.at[j],
            device(x, y_peers[j], z, core),
        ).wait_recv()
        upper = upper + came_ay[y_peers[NY - j]].astype(F32)
    lower = scatter_bz.result()
    answer = resid_ref[...].astype(F32) + jnp.concatenate([upper, lower], axis=0)
    answer = answer.astype(BF16)
    for j in range(NX):
        mixed[j] = answer[:, j * COLS : (j + 1) * COLS]
    for j in range(1, NX):
        copy = send_to(
            mixed.at[x_peers[j]],
            came_x.at[x],
            x_send.at[j],
            x_recv.at[j],
            device(x_peers[j], y, z, core),
        )
        copy.start()
        sent.append(copy)
    out_ref[pl.ds(pl.multiple_of(x * QUARTER, QUARTER), QUARTER), :] = mixed[x]
    for j in range(1, NX):
        source = x_peers[NX - j]
        send_to(
            mixed.at[x_peers[j]],
            came_x.at[source],
            x_send.at[j],
            x_recv.at[j],
            device(x_peers[j], y, z, core),
        ).wait_recv()
        out_ref[pl.ds(pl.multiple_of(source * QUARTER, QUARTER), QUARTER), :] = came_x[source]
    for copy in sent:
        copy.wait_send()
    for ring in (
        gather_az,
        gather_bz,
        gather_by,
        scatter_az,
        scatter_by,
        scatter_bz,
    ):
        for copy in ring.sent:
            copy.wait_send()


def shards(
    tokens,
    attn_gain,
    q_weight,
    key_matrix,
    value_matrix,
    o_weight,
    moe_gain,
    gate_weight,
    up_weight,
    down_weight,
    key_page_pool,
    value_page_pool,
    cache_lens,
    page_table,
    routes,
    route_gates,
):
    vmem = pl.BlockSpec(memory_space=pltpu.VMEM)
    smem = pl.BlockSpec(memory_space=pltpu.SMEM)
    hbm = pl.BlockSpec(memory_space=pl.ANY)
    dma = pltpu.SemaphoreType.DMA
    length = cache_lens[0]
    page = jnp.arange(CACHE // PAGE, dtype=jnp.int32)
    position = jnp.sum(jnp.where(page_table[0][None, :] == page[:, None], page[None, :], 0), axis=1)
    seen = length - position * PAGE
    half = HEAD // 2
    frequency = 10000.0 ** (-2.0 * jnp.arange(half, dtype=F32) / HEAD)
    places = (length + jnp.arange(ROWS, dtype=jnp.int32)).astype(F32)
    angle = places[:, None] * frequency
    cosine = jnp.tile(jnp.cos(angle), (1, 4))
    sine = jnp.sin(angle)
    sine = jnp.concatenate([-sine, sine, -sine, sine], axis=1)
    shape = jax.ShapeDtypeStruct
    gate_own, up_own, down_own = gate_weight[0], up_weight[0], down_weight[0]
    aug, resid, gate_all, up_all, down_all = pl.pallas_call(
        attend_kernel,
        out_shape=(
            shape((QUARTER, AUG), BF16),
            shape((QUARTER, WIDTH), BF16),
            shape((NX, WIDTH, 128), BF16),
            shape((NX, WIDTH, 128), BF16),
            shape((NX, 128, WIDTH), BF16),
        ),
        in_specs=[smem] + [vmem] * 7 + [hbm] * 9,
        out_specs=(vmem, vmem, hbm, hbm, hbm),
        scratch_shapes=[
            pltpu.VMEM((NX, ROWS, COLS), BF16),
            pltpu.VMEM((WIDTH, COLS), BF16),
            pltpu.VMEM((WIDTH, 128), BF16),
            pltpu.VMEM((WIDTH, 128), BF16),
            pltpu.VMEM((COLS, WIDTH), BF16),
            pltpu.VMEM((CACHE, 256), BF16),
            pltpu.VMEM((CACHE, 128), BF16),
            pltpu.VMEM((STACK, 256), BF16),
            pltpu.VMEM((STACK, 1), F32),
            pltpu.VMEM((STACK, 1), F32),
            pltpu.VMEM((STACK, 128), F32),
            pltpu.VMEM((NX, QUARTER, WIDTH), BF16),
            pltpu.VMEM((NX, QUARTER, WIDTH), BF16),
            pltpu.VMEM((NX, QUARTER, WIDTH), F32),
            dma((4,)),
            dma((BLOCKS,)),
            dma((BLOCKS,)),
            dma((NX,)),
            dma((NX,)),
            dma((NX,)),
            dma((NX,)),
            dma((6,)),
            dma((6,)),
        ],
        compiler_params=pltpu.CompilerParams(
            collective_id=0, has_side_effects=True, vmem_limit_bytes=60 << 20
        ),
        name="attend",
    )(
        seen,
        tokens,
        cosine,
        sine,
        routes,
        route_gates,
        attn_gain.reshape(1, WIDTH),
        moe_gain.reshape(1, WIDTH),
        q_weight,
        key_matrix,
        value_matrix,
        o_weight,
        key_page_pool.reshape(CACHE, 128),
        value_page_pool.reshape(CACHE, 128),
        gate_own,
        up_own,
        down_own,
    )
    pair = lambda *dims: pltpu.VMEM((2, *dims), BF16)
    return pl.pallas_call(
        expert_kernel,
        out_shape=shape((ROWS, COLS), BF16),
        in_specs=[hbm, vmem] + [hbm] * 6,
        out_specs=vmem,
        scratch_shapes=[
            pltpu.VMEM((NZ, NY, HALF, AUG), BF16),
            pltpu.VMEM((NY, NZ, HALF, AUG), BF16),
            pair(WIDTH, FFE),
            pair(WIDTH, FFE),
            pair(FFE, WIDTH),
            pltpu.VMEM((NZ, NY, HALF, WIDTH), F32),
            pltpu.VMEM((NY, NZ, HALF, WIDTH), F32),
            pltpu.VMEM((NY, HALF, WIDTH), F32),
            pltpu.VMEM((NZ, HALF, WIDTH), F32),
            pair(NZ // 2, NY, HALF, WIDTH),
            pair(NZ // 2, NY, HALF, WIDTH),
            pltpu.VMEM((NY, HALF, WIDTH), BF16),
            pltpu.VMEM((NY, HALF, WIDTH), BF16),
            pair(NY // 2, NZ, HALF, WIDTH),
            pair(NY // 2, NZ, HALF, WIDTH),
            pair(NZ // 2, HALF, WIDTH),
            pair(NZ // 2, HALF, WIDTH),
            pltpu.VMEM((NX, QUARTER, COLS), BF16),
            pltpu.VMEM((NX, QUARTER, COLS), BF16),
            dma((2,)),
            dma((3, 3)),
            dma((3, 2)),
            dma((3, 2)),
            dma((3, 4)),
            dma((3, 4)),
            dma((NY,)),
            dma((NY,)),
            dma((2, NZ // 2)),
            dma((2, NZ // 2)),
            dma((2, NY // 2)),
            dma((2, NY // 2)),
            dma((2, NZ // 2)),
            dma((2, NZ // 2)),
            dma((NY,)),
            dma((NY,)),
            dma((2, NZ // 2)),
            dma((2, NZ // 2)),
            dma((2, NY // 2)),
            dma((2, NY // 2)),
            dma((2, NZ // 2)),
            dma((2, NZ // 2)),
            dma((NX,)),
            dma((NX,)),
        ],
        compiler_params=pltpu.CompilerParams(
            collective_id=1, has_side_effects=True, vmem_limit_bytes=60 << 20
        ),
        name="experts",
    )(aug, resid, gate_own, up_own, down_own, gate_all, up_all, down_all)


def solution(mesh):
    in_specs = (
        P("seq", "tensor"),
        P(),
        P(None, "tensor"),
        P(None, "tensor"),
        P(None, "tensor"),
        P("tensor", None),
        P(),
        P("seq", None, "tensor"),
        P("seq", None, "tensor"),
        P("seq", "tensor", None),
        P("seq", None, "tensor"),
        P("seq", None, "tensor"),
        P("seq"),
        P("seq", None),
        P("seq", None),
        P("seq", None),
    )
    out_specs = P("seq", "tensor")
    return jax.shard_map(shards, mesh=mesh, in_specs=in_specs, out_specs=out_specs, check_vma=False)
```

```python
import jax
import jax.numpy as jnp
from jax import lax
from jax.experimental import pallas as pl
from jax.experimental.pallas import tpu as pltpu
from jax.sharding import PartitionSpec as P

MESH = pl.DeviceIdType.MESH
BF16 = jnp.bfloat16
F32 = jnp.float32
HEAD = 64
NORM_EPSILON = 1e-06
MASKED_SCORE = -1e30
NX, NY, NZ = 4, 4, 8
ROWS = 128
QUARTER = ROWS // NX
HALF = QUARTER // 2
WIDTH = 1536
COLS = WIDTH // NX
AUG = WIDTH + 128
HEADS = 6
STACK = HEADS * ROWS
CACHE = 8192
BLOCK = 1024
BLOCKS = CACHE // BLOCK
PAGE = 128
FFE = 512


def whereabouts():
    seq = lax.axis_index("seq")
    x = lax.axis_index("tensor")
    core = lax.rem(seq, 2)
    y = lax.rem(lax.div(seq, 2), NY)
    z = lax.div(seq, 2 * NY)
    return x, y, z, core


def device(x, y, z, core):
    return ((z * NY + y) * 2 + core, x)


def send_to(src, dst, send_sem, recv_sem, target):
    return pltpu.make_async_remote_copy(
        src_ref=src,
        dst_ref=dst,
        send_sem=send_sem,
        recv_sem=recv_sem,
        device_id=target,
        device_id_type=MESH,
    )


def greet(targets):
    barrier = pltpu.get_barrier_semaphore()
    for target in targets:
        pl.semaphore_signal(barrier, inc=1, device_id=target, device_id_type=MESH)
    pl.semaphore_wait(barrier, len(targets))


def norm_rows(widened, gain_row):
    return (
        widened
        * lax.rsqrt(jnp.mean(widened * widened, axis=1, keepdims=True) + NORM_EPSILON)
        * gain_row
    )


def swap_halves(block):
    lane = lax.broadcasted_iota(jnp.int32, block.shape, 1)
    return jnp.where(
        lax.rem(lane, HEAD) < HEAD // 2,
        pltpu.roll(block, 128 - HEAD // 2, 1),
        pltpu.roll(block, HEAD // 2, 1),
    )


class Gather:
    def __init__(self, size, me, target, place, halves, send_sem, recv_sem):
        self.size, self.me, self.target = size, me, target
        self.place, self.halves = place, halves
        self.send_sem, self.recv_sem = send_sem, recv_sem
        self.sent = []

    def copies(self, k, arriving):
        last = k + 1 == self.size // 2
        made = []
        for way in range(2):
            if arriving:
                shift = -(1 + k) if way == 0 else 1 + k
            else:
                shift = -k if way == 0 else k
            ref = self.place(lax.rem(self.me + shift + self.size, self.size))
            if last:
                ref = self.halves(ref)[way]
            made.append(
                send_to(
                    ref,
                    ref,
                    self.send_sem.at[way, k],
                    self.recv_sem.at[way, k],
                    self.target(1 if way == 0 else -1),
                )
            )
        return made

    def send(self, k):
        for copy in self.copies(k, False):
            copy.start()
            self.sent.append(copy)

    def wait(self, k):
        for copy in self.copies(k, True):
            copy.wait_recv()


class Scatter:
    def __init__(self, size, me, target, own, halves, stage, arrived, send_sem, recv_sem):
        self.size, self.me, self.target = size, me, target
        self.own, self.halves = own, halves
        self.stage, self.arrived = stage, arrived
        self.send_sem, self.recv_sem = send_sem, recv_sem
        self.sent = []

    def copy(self, way, k):
        src, dst = self.stage.at[way, k], self.arrived.at[way, k]
        if k == 0:
            src, dst = self.halves(src)[way], self.halves(dst)[way]
        return send_to(
            src,
            dst,
            self.send_sem.at[way, k],
            self.recv_sem.at[way, k],
            self.target(1 if way == 0 else -1),
        )

    def send(self, k):
        distance = self.size // 2 - k
        for way in range(2):
            shift = distance if way == 0 else -distance
            own = self.own(lax.rem(self.me + shift + self.size, self.size))
            here = self.stage.at[way, k]
            if k == 0:
                self.halves(here)[way][...] = self.halves(own)[way][...].astype(BF16)
            elif k == 1:
                self.copy(way, 0).wait_recv()
                came = self.halves(self.arrived.at[way, 0])[way]
                self.halves(here)[way][...] = (
                    self.halves(own)[way][...] + came[...].astype(F32)
                ).astype(BF16)
                self.halves(here)[1 - way][...] = self.halves(own)[1 - way][...].astype(BF16)
            else:
                self.copy(way, k - 1).wait_recv()
                here[...] = (own[...] + self.arrived[way, k - 1].astype(F32)).astype(BF16)
            copy = self.copy(way, k)
            copy.start()
            self.sent.append(copy)

    def result(self):
        k = self.size // 2 - 1
        answer = self.own(self.me)[...]
        for way in range(2):
            self.copy(way, k).wait_recv()
            answer = answer + self.arrived[way, k].astype(F32)
        return answer


def half_columns(ref):
    width = ref.shape[-1]
    split = (width // 256 + (width // 128) % 2) * 128
    lead = (slice(None),) * (len(ref.shape) - 1)
    return (
        ref.at[(*lead, pl.ds(0, split))],
        ref.at[(*lead, pl.ds(split, width - split))],
    )


def half_rows(ref):
    size = ref.shape[0] // 2
    return ref.at[pl.ds(0, size)], ref.at[pl.ds(size, size)]


def layer_kernel(
    length_ref,
    table_ref,
    tokens_ref,
    cos_ref,
    sin_ref,
    routes_ref,
    gates_ref,
    attn_gain_ref,
    moe_gain_ref,
    q_hbm,
    k_hbm,
    v_hbm,
    o_hbm,
    key_pool,
    value_pool,
    gate_hbm,
    up_hbm,
    down_hbm,
    out_ref,
    tok,
    qw,
    kw,
    vw,
    ow,
    keys,
    values,
    stacked,
    best,
    total,
    mix,
    stage,
    arrived,
    partial,
    route_rows,
    resid,
    rows_a,
    rows_b,
    wg,
    wu,
    wd,
    out_a,
    out_b,
    sum_a,
    sum_b,
    stage_az,
    came_az,
    stage_ay,
    came_ay,
    stage_by,
    came_by,
    stage_bz,
    came_bz,
    mixed,
    came_x,
    load_sem,
    key_sem,
    value_sem,
    tok_send,
    tok_recv,
    sum_send,
    sum_recv,
    own_sem,
    near_send,
    near_recv,
    far_send,
    far_recv,
    part_send,
    part_recv,
    ay_send,
    ay_recv,
    az_send,
    az_recv,
    by_send,
    by_recv,
    bz_send,
    bz_recv,
    ry_send,
    ry_recv,
    raz_send,
    raz_recv,
    rby_send,
    rby_recv,
    rbz_send,
    rbz_recv,
    x_send,
    x_recv,
):
    x, y, z, core = whereabouts()
    peers = [lax.rem(x + j, NX) for j in range(NX)]
    y_peers = [lax.rem(y + j, NY) for j in range(NY)]
    z_at = lambda step: lax.rem(z + step + NZ, NZ)
    partner = device(x, y, z, 1 - core)
    sent = []
    loads = []
    for number, (src, dst) in enumerate(
        ((q_hbm, qw), (k_hbm, kw), (v_hbm, vw), (o_hbm, ow))
    ):
        copy = pltpu.make_async_copy(src, dst, load_sem.at[number])
        copy.start()
        loads.append(copy)

    def key_copy(i):
        rows = pl.ds(pl.multiple_of(i * BLOCK, BLOCK), BLOCK)
        return pltpu.make_async_copy(
            key_pool.at[rows, :], keys.at[rows, pl.ds(0, 128)], key_sem.at[i]
        )

    def value_copy(i):
        rows = pl.ds(pl.multiple_of(i * BLOCK, BLOCK), BLOCK)
        return pltpu.make_async_copy(
            value_pool.at[rows, :], values.at[rows, :], value_sem.at[i]
        )

    for i in range(BLOCKS):
        key_copy(i).start()
        value_copy(i).start()

    greet(
        [device(peers[j], y, z, core) for j in range(1, NX)]
        + [device(x, y_peers[j], z, core) for j in range(1, NY)]
        + [device(x, y, z_at(1), core), device(x, y, z_at(-1), core), partner]
    )
    for j in range(1, NX):
        copy = send_to(
            tokens_ref,
            tok.at[x],
            tok_send.at[j],
            tok_recv.at[j],
            device(peers[j], y, z, core),
        )
        copy.start()
        sent.append(copy)
    tok[x] = tokens_ref[...]

    weights = ((gate_hbm, wg), (up_hbm, wu), (down_hbm, wd))

    def part_of(number, owner, q, way=None):
        w = weights[number][1]
        size = (128 if number == 2 else WIDTH) // (1 if way is None else 2)
        first = 0 if way is None else way * size
        if number == 2:
            return w.at[owner, pl.ds(pl.multiple_of(q * 128 + first, 64), size), :]
        return w.at[owner, pl.ds(first, size), pl.ds(pl.multiple_of(q * 128, 128), 128)]

    def own_copy(number):
        return pltpu.make_async_copy(
            weights[number][0], part_of(number, core, x), own_sem.at[number]
        )

    def near_copy(number, way, q):
        return send_to(
            weights[number][0],
            part_of(number, core, q),
            near_send.at[number, way],
            near_recv.at[number, way],
            device(peers[(1, NX - 1)[way]], y, z, core),
        )

    def far_copy(number, way, q):
        place = part_of(number, core, q, way)
        return send_to(
            place,
            place,
            far_send.at[number, way],
            far_recv.at[number, way],
            device(peers[(1, NX - 1)[way]], y, z, core),
        )

    def part_copy(number, which, owner, src=None):
        place = part_of(number, owner, peers[which])
        return send_to(
            place if src is None else src,
            place,
            part_send.at[number, which],
            part_recv.at[number, which],
            partner,
        )

    def begin(copy):
        copy.start()
        sent.append(copy)

    def send_near(number):
        own_copy(number).start()
        for way in range(2):
            begin(near_copy(number, way, x))
        begin(part_copy(number, 0, core, weights[number][0]))

    def send_far(number):
        for way, q in ((0, peers[NX - 1]), (1, peers[1])):
            near_copy(number, way, q).wait_recv()
            begin(far_copy(number, way, q))
        begin(part_copy(number, 1, core))
        begin(part_copy(number, NX - 1, core))

    def share_far(number):
        for way in range(2):
            far_copy(number, way, peers[2]).wait_recv()
        begin(part_copy(number, 2, core))

    def settle(number):
        own_copy(number).wait()
        for which in range(NX):
            part_copy(number, which, 1 - core).wait_recv()

    send_near(0)
    send_near(1)

    row = lax.broadcasted_iota(jnp.int32, (PAGE, 128), 0)
    lane = lax.broadcasted_iota(jnp.int32, (PAGE, 128), 1)
    pages = CACHE // PAGE
    pool_page = lax.broadcasted_iota(jnp.int32, (pages, pages), 0)
    cache_page = lax.broadcasted_iota(jnp.int32, (pages, pages), 1)
    position = jnp.sum(
        jnp.where(table_ref[...] == pool_page, cache_page, 0).astype(F32),
        axis=1,
        keepdims=True,
    ).astype(jnp.int32)
    seen = length_ref[0] - position * PAGE
    for p in range(pages):
        hidden_row = (lane == 0) & (row >= seen[p : p + 1, :])
        keys[p * PAGE : (p + 1) * PAGE, 128:256] = jnp.where(
            hidden_row, MASKED_SCORE, 0.0
        ).astype(BF16)

    expert = lax.rem(row, 64)
    chosen = jnp.zeros((128, ROWS), F32)
    for k in range(routes_ref.shape[0]):
        chosen = chosen + jnp.where(
            routes_ref[k : k + 1, :] == expert, gates_ref[k : k + 1, :], 0.0
        )
    high_part = chosen.astype(BF16).astype(F32)
    route_rows[...] = jnp.where(row >= 64, chosen - high_part, high_part).T

    for j in range(1, NX):
        send_to(
            tokens_ref,
            tok.at[peers[NX - j]],
            tok_send.at[j],
            tok_recv.at[j],
            device(peers[j], y, z, core),
        ).wait_recv()
    whole = jnp.concatenate([tok[j].astype(F32) for j in range(NX)], axis=1)
    normed = norm_rows(whole, attn_gain_ref[...].reshape(1, WIDTH)).astype(BF16)
    for copy in loads:
        copy.wait()
    cosine = cos_ref[...]
    sine = sin_ref[...]
    scale = HEAD ** (-0.5)
    queries = jnp.dot(normed, qw[...], preferred_element_type=F32)
    first_bias = jnp.where(lane == 0, 1.0, 0.0).astype(BF16)
    for pair in range(HEADS // 2):
        block = queries[:, pair * 128 : (pair + 1) * 128]
        turned = (block * cosine + swap_halves(block) * sine).astype(BF16)
        turned = turned.astype(F32) * scale
        crossed = pltpu.roll(turned, HEAD, 1)
        for side in range(2):
            head = 2 * pair + side
            group = head // 3
            placed = turned if side == group else crossed
            mine = (lane < HEAD) if group == 0 else (lane >= HEAD)
            stacked[pl.ds(head * ROWS, ROWS), pl.ds(0, 128)] = jnp.where(
                mine, placed, 0.0
            ).astype(BF16)
            stacked[pl.ds(head * ROWS, ROWS), pl.ds(128, 128)] = first_bias
    new_keys = jnp.dot(normed, kw[...], preferred_element_type=F32)
    new_keys = (new_keys * cosine + swap_halves(new_keys) * sine).astype(BF16)
    new_values = jnp.dot(normed, vw[...], preferred_element_type=F32).astype(BF16)

    scores = lax.dot_general(
        stacked[:, 0:128],
        new_keys,
        (((1,), (1,)), ((), ())),
        preferred_element_type=F32,
    )
    query_row = lax.rem(lax.broadcasted_iota(jnp.int32, (STACK, ROWS), 0), ROWS)
    key_row = lax.broadcasted_iota(jnp.int32, (STACK, ROWS), 1)
    scores = jnp.where(key_row <= query_row, scores, MASKED_SCORE)
    top = jnp.max(scores, axis=1, keepdims=True)
    odds = jnp.exp(scores - top)
    best[...] = top
    total[...] = jnp.sum(odds, axis=1, keepdims=True)
    mix[...] = jnp.dot(odds.astype(BF16), new_values, preferred_element_type=F32)

    def step(i, carry):
        key_copy(i).wait()
        value_copy(i).wait()
        rows = pl.ds(pl.multiple_of(i * BLOCK, BLOCK), BLOCK)
        scores = lax.dot_general(
            stacked[...],
            keys[rows, :],
            (((1,), (1,)), ((), ())),
            preferred_element_type=F32,
        )
        old = best[...]
        new = jnp.maximum(old, jnp.max(scores, axis=1, keepdims=True))
        shrink = jnp.exp(old - new)
        odds = jnp.exp(scores - new)
        best[...] = new
        total[...] = total[...] * shrink + jnp.sum(odds, axis=1, keepdims=True)
        mix[...] = mix[...] * shrink + jnp.dot(
            odds.astype(BF16), values[rows, :], preferred_element_type=F32
        )
        return carry

    lax.fori_loop(0, 4, step, 0)
    send_far(0)
    send_near(2)
    lax.fori_loop(4, 7, step, 0)
    send_far(1)
    lax.fori_loop(7, BLOCKS, step, 0)
    result = mix[...] / total[...]
    pieces = []
    for pair in range(HEADS // 2):
        sides = []
        for side in range(2):
            head = 2 * pair + side
            block = result[head * ROWS : (head + 1) * ROWS, :]
            sides.append(block if side == head // 3 else pltpu.roll(block, HEAD, 1))
        pieces.append(jnp.where(lane < HEAD, sides[0], sides[1]).astype(BF16))
    attended = jnp.concatenate(pieces, axis=1)
    summand = jnp.dot(attended, ow[...], preferred_element_type=F32)
    for j in range(NX):
        quarter = summand[j * QUARTER : (j + 1) * QUARTER, :]
        partial[j] = quarter
        stage[j] = quarter.astype(BF16)
    for j in range(1, NX):
        copy = send_to(
            stage.at[peers[j]],
            arrived.at[x],
            sum_send.at[j],
            sum_recv.at[j],
            device(peers[j], y, z, core),
        )
        copy.start()
        sent.append(copy)

    my_rows = pl.ds(pl.multiple_of(x * QUARTER, QUARTER), QUARTER)
    residual = partial[x] + jnp.concatenate(
        [tok[j, my_rows, :].astype(F32) for j in range(NX)], axis=1
    )
    for j in range(1, NX):
        send_to(
            stage.at[peers[j]],
            arrived.at[peers[NX - j]],
            sum_send.at[j],
            sum_recv.at[j],
            device(peers[j], y, z, core),
        ).wait_recv()
        residual = residual + arrived[peers[NX - j]].astype(F32)
    residual = residual.astype(BF16)
    resid[...] = residual
    moe_in = norm_rows(residual.astype(F32), moe_gain_ref[...].reshape(1, WIDTH)).astype(BF16)
    augmented = jnp.concatenate([moe_in, route_rows[my_rows, :].astype(BF16)], axis=1)
    rows_a[z, y] = augmented[0:HALF]
    rows_b[y, z] = augmented[HALF:QUARTER]

    for j in range(1, NY):
        begin(
            send_to(
                rows_a.at[z, y],
                rows_a.at[z, y],
                ay_send.at[j],
                ay_recv.at[j],
                device(x, y_peers[j], z, core),
            )
        )
    to_z = lambda step: device(x, y, z_at(step), core)
    to_y = lambda step: device(x, y_peers[step % NY], z, core)
    gather_az = Gather(NZ, z, to_z, lambda i: rows_a.at[i], half_rows, az_send, az_recv)
    gather_bz = Gather(NZ, z, to_z, lambda i: rows_b.at[y, i], half_columns, bz_send, bz_recv)
    gather_by = Gather(NY, y, to_y, lambda i: rows_b.at[i], half_rows, by_send, by_recv)
    gather_bz.send(0)
    share_far(0)
    send_far(2)
    for j in range(1, NY):
        place = rows_a.at[z, y_peers[NY - j]]
        send_to(
            place, place, ay_send.at[j], ay_recv.at[j], device(x, y_peers[j], z, core)
        ).wait_recv()
    gather_az.send(0)
    gather_bz.wait(0)
    gather_bz.send(1)
    gather_bz.wait(1)
    gather_bz.send(2)
    gather_az.wait(0)
    gather_az.send(1)
    gather_bz.wait(2)
    gather_bz.send(3)
    gather_bz.wait(3)
    gather_by.send(0)
    share_far(1)
    gather_az.wait(1)
    gather_az.send(2)
    share_far(2)
    for number in range(3):
        settle(number)

    first_expert = 2 * (z * NY + y)

    def compute(rows, out, places):
        lead = rows.shape[1] * rows.shape[2]
        count = lead * len(places)
        block = jnp.concatenate([rows[i].reshape(lead, AUG) for i in places], axis=0)
        inputs = block[:, 0:WIDTH]
        gates = block[:, WIDTH:AUG].astype(F32)
        number = lax.rem(lax.broadcasted_iota(jnp.int32, (count, 128), 1), 64)
        answer = None
        for e in range(2):
            gate = jnp.sum(
                jnp.where(number == first_expert + e, gates, 0.0), axis=1, keepdims=True
            )
            gate_act = jnp.dot(inputs, wg[e], preferred_element_type=F32)
            up_act = jnp.dot(inputs, wu[e], preferred_element_type=F32)
            hidden = (gate_act / (1.0 + jnp.exp(-gate_act)) * up_act * gate).astype(BF16)
            term = jnp.dot(hidden, wd[e], preferred_element_type=F32)
            answer = term if answer is None else answer + term
        for at, i in enumerate(places):
            out[i] = answer[at * lead : (at + 1) * lead].reshape(
                rows.shape[1], rows.shape[2], WIDTH
            )

    scatter_az = Scatter(
        NZ, z, to_z, lambda i: out_a.at[i], half_rows, stage_az, came_az, raz_send, raz_recv
    )
    scatter_by = Scatter(
        NY, y, to_y, lambda i: out_b.at[i], half_rows, stage_by, came_by, rby_send, rby_recv
    )
    scatter_bz = Scatter(
        NZ, z, to_z, lambda i: sum_b.at[i], half_columns, stage_bz, came_bz, rbz_send, rbz_recv
    )
    compute(rows_a, out_a, [z, z_at(1), z_at(-1), z_at(2)])
    gather_az.wait(2)
    gather_az.send(3)
    gather_by.wait(0)
    gather_by.send(1)
    compute(rows_b, out_b, [y, y_peers[1]])
    gather_az.wait(3)
    compute(rows_a, out_a, [z_at(4), z_at(3), z_at(-3), z_at(-2)])
    scatter_az.send(0)
    gather_by.wait(1)
    compute(rows_b, out_b, [y_peers[2], y_peers[3]])
    scatter_by.send(0)
    scatter_az.send(1)
    scatter_by.send(1)
    scatter_az.send(2)
    scatter_az.send(3)
    sum_b[...] = scatter_by.result()
    scatter_bz.send(0)
    sum_a[...] = scatter_az.result()
    stage_ay[...] = sum_a[...].astype(BF16)
    for j in range(1, NY):
        copy = send_to(
            stage_ay.at[y_peers[j]],
            came_ay.at[y],
            ry_send.at[j],
            ry_recv.at[j],
            device(x, y_peers[j], z, core),
        )
        copy.start()
        sent.append(copy)
    scatter_bz.send(1)
    scatter_bz.send(2)
    scatter_bz.send(3)
    upper = sum_a[y]
    for j in range(1, NY):
        send_to(
            stage_ay.at[y_peers[j]],
            came_ay.at[y_peers[NY - j]],
            ry_send.at[j],
            ry_recv.at[j],
            device(x, y_peers[j], z, core),
        ).wait_recv()
        upper = upper + came_ay[y_peers[NY - j]].astype(F32)
    lower = scatter_bz.result()
    answer = resid[...].astype(F32) + jnp.concatenate([upper, lower], axis=0)
    answer = answer.astype(BF16)
    for j in range(NX):
        mixed[j] = answer[:, j * COLS : (j + 1) * COLS]
    for j in range(1, NX):
        copy = send_to(
            mixed.at[peers[j]],
            came_x.at[x],
            x_send.at[j],
            x_recv.at[j],
            device(peers[j], y, z, core),
        )
        copy.start()
        sent.append(copy)
    out_ref[pl.ds(pl.multiple_of(x * QUARTER, QUARTER), QUARTER), :] = mixed[x]
    for j in range(1, NX):
        source = peers[NX - j]
        send_to(
            mixed.at[peers[j]],
            came_x.at[source],
            x_send.at[j],
            x_recv.at[j],
            device(peers[j], y, z, core),
        ).wait_recv()
        out_ref[pl.ds(pl.multiple_of(source * QUARTER, QUARTER), QUARTER), :] = came_x[source]
    for copy in sent:
        copy.wait_send()
    for ring in (
        gather_az,
        gather_bz,
        gather_by,
        scatter_az,
        scatter_by,
        scatter_bz,
    ):
        for copy in ring.sent:
            copy.wait_send()


def shards(
    tokens,
    attn_gain,
    q_weight,
    key_matrix,
    value_matrix,
    o_weight,
    moe_gain,
    gate_weight,
    up_weight,
    down_weight,
    key_page_pool,
    value_page_pool,
    cache_lens,
    page_table,
    routes,
    route_gates,
):
    vmem = pl.BlockSpec(memory_space=pltpu.VMEM)
    smem = pl.BlockSpec(memory_space=pltpu.SMEM)
    hbm = pl.BlockSpec(memory_space=pl.ANY)
    dma = pltpu.SemaphoreType.DMA
    length = cache_lens[0]
    places = (length + jnp.arange(ROWS, dtype=jnp.int32)).astype(F32)
    entry = jnp.arange(128, dtype=jnp.int32) % HEAD
    frequency = 10000.0 ** (-2.0 * (entry % (HEAD // 2)).astype(F32) / HEAD)
    angle = places[:, None] * frequency
    cosine = jnp.cos(angle)
    sine = jnp.where(entry < HEAD // 2, -1.0, 1.0) * jnp.sin(angle)
    shape = jax.ShapeDtypeStruct
    pair = lambda *dims: pltpu.VMEM((2, *dims), BF16)
    both = lambda *dims: [dma(dims), dma(dims)]
    return pl.pallas_call(
        layer_kernel,
        out_shape=shape((ROWS, COLS), BF16),
        in_specs=[smem] + [vmem] * 8 + [hbm] * 9,
        out_specs=vmem,
        scratch_shapes=[
            pltpu.VMEM((NX, ROWS, COLS), BF16),
            pltpu.VMEM((WIDTH, COLS), BF16),
            pltpu.VMEM((WIDTH, 128), BF16),
            pltpu.VMEM((WIDTH, 128), BF16),
            pltpu.VMEM((COLS, WIDTH), BF16),
            pltpu.VMEM((CACHE, 256), BF16),
            pltpu.VMEM((CACHE, 128), BF16),
            pltpu.VMEM((STACK, 256), BF16),
            pltpu.VMEM((STACK, 1), F32),
            pltpu.VMEM((STACK, 1), F32),
            pltpu.VMEM((STACK, 128), F32),
            pltpu.VMEM((NX, QUARTER, WIDTH), BF16),
            pltpu.VMEM((NX, QUARTER, WIDTH), BF16),
            pltpu.VMEM((NX, QUARTER, WIDTH), F32),
            pltpu.VMEM((ROWS, 128), F32),
            pltpu.VMEM((QUARTER, WIDTH), BF16),
            pltpu.VMEM((NZ, NY, HALF, AUG), BF16),
            pltpu.VMEM((NY, NZ, HALF, AUG), BF16),
            pair(WIDTH, FFE),
            pair(WIDTH, FFE),
            pair(FFE, WIDTH),
            pltpu.VMEM((NZ, NY, HALF, WIDTH), F32),
            pltpu.VMEM((NY, NZ, HALF, WIDTH), F32),
            pltpu.VMEM((NY, HALF, WIDTH), F32),
            pltpu.VMEM((NZ, HALF, WIDTH), F32),
            pair(NZ // 2, NY, HALF, WIDTH),
            pair(NZ // 2, NY, HALF, WIDTH),
            pltpu.VMEM((NY, HALF, WIDTH), BF16),
            pltpu.VMEM((NY, HALF, WIDTH), BF16),
            pair(NY // 2, NZ, HALF, WIDTH),
            pair(NY // 2, NZ, HALF, WIDTH),
            pair(NZ // 2, HALF, WIDTH),
            pair(NZ // 2, HALF, WIDTH),
            pltpu.VMEM((NX, QUARTER, COLS), BF16),
            pltpu.VMEM((NX, QUARTER, COLS), BF16),
            dma((4,)),
            dma((BLOCKS,)),
            dma((BLOCKS,)),
            *both(NX),
            *both(NX),
            dma((3,)),
            *both(3, 2),
            *both(3, 2),
            *both(3, NX),
            *both(NY),
            *both(2, NZ // 2),
            *both(2, NY // 2),
            *both(2, NZ // 2),
            *both(NY),
            *both(2, NZ // 2),
            *both(2, NY // 2),
            *both(2, NZ // 2),
            *both(NX),
        ],
        compiler_params=pltpu.CompilerParams(
            collective_id=0, has_side_effects=True, vmem_limit_bytes=62 << 20
        ),
        name="layer",
    )(
        cache_lens,
        page_table,
        tokens,
        cosine,
        sine,
        routes.T,
        route_gates.T,
        attn_gain,
        moe_gain,
        q_weight,
        key_matrix,
        value_matrix,
        o_weight,
        key_page_pool.reshape(CACHE, 128),
        value_page_pool.reshape(CACHE, 128),
        gate_weight[0],
        up_weight[0],
        down_weight[0],
    )


def solution(mesh):
    in_specs = (
        P("seq", "tensor"),
        P(),
        P(None, "tensor"),
        P(None, "tensor"),
        P(None, "tensor"),
        P("tensor", None),
        P(),
        P("seq", None, "tensor"),
        P("seq", None, "tensor"),
        P("seq", "tensor", None),
        P("seq", None, "tensor"),
        P("seq", None, "tensor"),
        P("seq"),
        P("seq", None),
        P("seq", None),
        P("seq", None),
    )
    out_specs = P("seq", "tensor")
    return jax.shard_map(shards, mesh=mesh, in_specs=in_specs, out_specs=out_specs, check_vma=False)
```

```python
import jax
import jax.numpy as jnp
from jax import lax
from jax.experimental import pallas as pl
from jax.experimental.pallas import tpu as pltpu
from jax.sharding import PartitionSpec as P

MESH = pl.DeviceIdType.MESH
BF16 = jnp.bfloat16
F32 = jnp.float32
HEAD = 64
NORM_EPSILON = 1e-06
MASKED_SCORE = -1e30
NX, NY, NZ = 4, 4, 8
ROWS = 128
QUARTER = ROWS // NX
HALF = QUARTER // 2
WIDTH = 1536
COLS = WIDTH // NX
AUG = WIDTH + 128
HEADS = 6
STACK = HEADS * ROWS
CACHE = 8192
BLOCK = 1024
BLOCKS = CACHE // BLOCK
PAGE = 128
FFE = 512


def whereabouts():
    seq = lax.axis_index("seq")
    x = lax.axis_index("tensor")
    core = lax.rem(seq, 2)
    y = lax.rem(lax.div(seq, 2), NY)
    z = lax.div(seq, 2 * NY)
    return x, y, z, core


def device(x, y, z, core):
    return ((z * NY + y) * 2 + core, x)


def send_to(src, dst, send_sem, recv_sem, target):
    return pltpu.make_async_remote_copy(
        src_ref=src,
        dst_ref=dst,
        send_sem=send_sem,
        recv_sem=recv_sem,
        device_id=target,
        device_id_type=MESH,
    )


def greet(targets):
    barrier = pltpu.get_barrier_semaphore()
    for target in targets:
        pl.semaphore_signal(barrier, inc=1, device_id=target, device_id_type=MESH)
    pl.semaphore_wait(barrier, len(targets))


def norm_rows(widened, gain_row):
    return (
        widened
        * lax.rsqrt(jnp.mean(widened * widened, axis=1, keepdims=True) + NORM_EPSILON)
        * gain_row
    )


def swap_halves(block):
    lane = lax.broadcasted_iota(jnp.int32, block.shape, 1)
    return jnp.where(
        lax.rem(lane, HEAD) < HEAD // 2,
        pltpu.roll(block, 128 - HEAD // 2, 1),
        pltpu.roll(block, HEAD // 2, 1),
    )


class Gather:
    def __init__(self, size, me, target, place, parts, send_sem, recv_sem):
        self.size, self.me, self.target = size, me, target
        self.place, self.parts = place, parts
        self.send_sem, self.recv_sem = send_sem, recv_sem
        self.sent = []

    def copies(self, k, s, arriving):
        last = k + 1 == self.size // 2
        made = []
        for way in range(2):
            if last and self.parts > 1 and s // (self.parts // 2) != way:
                continue
            if arriving:
                shift = -(1 + k) if way == 0 else 1 + k
            else:
                shift = -k if way == 0 else k
            ref = self.place(lax.rem(self.me + shift + self.size, self.size), s)
            if last and self.parts == 1:
                ref = half_columns(ref)[way]
            made.append(
                send_to(
                    ref,
                    ref,
                    self.send_sem.at[way, k, s],
                    self.recv_sem.at[way, k, s],
                    self.target(1 if way == 0 else -1),
                )
            )
        return made

    def send(self, k, s=0):
        for copy in self.copies(k, s, False):
            copy.start()
            self.sent.append(copy)

    def wait(self, k, s=0):
        for copy in self.copies(k, s, True):
            copy.wait_recv()

    def relay(self, k, *parts):
        for s in parts:
            self.wait(k, s)
            self.send(k + 1, s)


class Scatter:
    def __init__(self, size, me, target, own, parts, stage, arrived, send_sem, recv_sem):
        self.size, self.me, self.target = size, me, target
        self.own, self.parts = own, parts
        self.stage, self.arrived = stage, arrived
        self.send_sem, self.recv_sem = send_sem, recv_sem
        self.sent = []

    def copy(self, way, k, s):
        src, dst = self.stage.at[way, k, s], self.arrived.at[way, k, s]
        if k == 0 and self.parts == 1:
            src, dst = half_columns(src)[way], half_columns(dst)[way]
        return send_to(
            src,
            dst,
            self.send_sem.at[way, k, s],
            self.recv_sem.at[way, k, s],
            self.target(1 if way == 0 else -1),
        )

    def send(self, k, s=0):
        distance = self.size // 2 - k
        for way in range(2):
            mine = self.parts == 1 or s // (self.parts // 2) == way
            if k == 0 and not mine:
                continue
            shift = distance if way == 0 else -distance
            own = self.own(lax.rem(self.me + shift + self.size, self.size), s)
            here = self.stage.at[way, k, s]
            if k == 0 and self.parts == 1:
                half_columns(here)[way][...] = half_columns(own)[way][...].astype(BF16)
            elif k == 0 or (k == 1 and not mine):
                here[...] = own[...].astype(BF16)
            elif k == 1 and self.parts == 1:
                self.copy(way, 0, s).wait_recv()
                came = half_columns(self.arrived.at[way, 0, s])[way]
                half_columns(here)[way][...] = (
                    half_columns(own)[way][...] + came[...].astype(F32)
                ).astype(BF16)
                half_columns(here)[1 - way][...] = half_columns(own)[1 - way][...].astype(BF16)
            else:
                self.copy(way, k - 1, s).wait_recv()
                here[...] = (own[...] + self.arrived[way, k - 1, s].astype(F32)).astype(BF16)
            copy = self.copy(way, k, s)
            copy.start()
            self.sent.append(copy)

    def result(self, s=0):
        k = self.size // 2 - 1
        answer = self.own(self.me, s)[...]
        for way in range(2):
            self.copy(way, k, s).wait_recv()
            answer = answer + self.arrived[way, k, s].astype(F32)
        return answer


def half_columns(ref):
    width = ref.shape[-1]
    split = (width // 256 + (width // 128) % 2) * 128
    lead = (slice(None),) * (len(ref.shape) - 1)
    return (
        ref.at[(*lead, pl.ds(0, split))],
        ref.at[(*lead, pl.ds(split, width - split))],
    )


def layer_kernel(
    length_ref,
    table_ref,
    tokens_ref,
    cos_ref,
    sin_ref,
    routes_ref,
    gates_ref,
    attn_gain_ref,
    moe_gain_ref,
    q_hbm,
    k_hbm,
    v_hbm,
    o_hbm,
    key_pool,
    value_pool,
    gate_hbm,
    up_hbm,
    down_hbm,
    out_ref,
    tok,
    qw,
    kw,
    vw,
    ow,
    keys,
    values,
    stacked,
    best,
    total,
    mix,
    stage,
    arrived,
    partial,
    route_rows,
    resid,
    rows_a,
    rows_b,
    wg,
    wu,
    wd,
    out_a,
    out_b,
    sum_b,
    stage_az,
    came_az,
    stage_ay,
    came_ay,
    stage_by,
    came_by,
    stage_bz,
    came_bz,
    mixed,
    came_x,
    load_sem,
    key_sem,
    value_sem,
    tok_send,
    tok_recv,
    sum_send,
    sum_recv,
    own_sem,
    near_send,
    near_recv,
    far_send,
    far_recv,
    part_send,
    part_recv,
    ay_send,
    ay_recv,
    az_send,
    az_recv,
    by_send,
    by_recv,
    bz_send,
    bz_recv,
    ry_send,
    ry_recv,
    raz_send,
    raz_recv,
    rby_send,
    rby_recv,
    rbz_send,
    rbz_recv,
    x_send,
    x_recv,
):
    x, y, z, core = whereabouts()
    peers = [lax.rem(x + j, NX) for j in range(NX)]
    y_peers = [lax.rem(y + j, NY) for j in range(NY)]
    z_at = lambda step: lax.rem(z + step + NZ, NZ)
    partner = device(x, y, z, 1 - core)
    sent = []
    loads = []
    for number, (src, dst) in enumerate(
        ((q_hbm, qw), (k_hbm, kw), (v_hbm, vw), (o_hbm, ow))
    ):
        copy = pltpu.make_async_copy(src, dst, load_sem.at[number])
        copy.start()
        loads.append(copy)

    def key_copy(i):
        rows = pl.ds(pl.multiple_of(i * BLOCK, BLOCK), BLOCK)
        return pltpu.make_async_copy(
            key_pool.at[rows, :], keys.at[rows, pl.ds(0, 128)], key_sem.at[i]
        )

    def value_copy(i):
        rows = pl.ds(pl.multiple_of(i * BLOCK, BLOCK), BLOCK)
        return pltpu.make_async_copy(
            value_pool.at[rows, :], values.at[rows, :], value_sem.at[i]
        )

    for i in range(BLOCKS):
        key_copy(i).start()
        value_copy(i).start()

    greet(
        [device(peers[j], y, z, core) for j in range(1, NX)]
        + [device(x, y_peers[j], z, core) for j in range(1, NY)]
        + [device(x, y, z_at(1), core), device(x, y, z_at(-1), core), partner]
    )
    for j in range(1, NX):
        copy = send_to(
            tokens_ref,
            tok.at[x],
            tok_send.at[j],
            tok_recv.at[j],
            device(peers[j], y, z, core),
        )
        copy.start()
        sent.append(copy)
    tok[x] = tokens_ref[...]

    weights = ((gate_hbm, wg), (up_hbm, wu), (down_hbm, wd))

    def part_of(number, owner, q, way=None):
        w = weights[number][1]
        size = (128 if number == 2 else WIDTH) // (1 if way is None else 2)
        first = 0 if way is None else way * size
        if number == 2:
            return w.at[owner, pl.ds(pl.multiple_of(q * 128 + first, 64), size), :]
        return w.at[owner, pl.ds(first, size), pl.ds(pl.multiple_of(q * 128, 128), 128)]

    def own_copy(number):
        return pltpu.make_async_copy(
            weights[number][0], part_of(number, core, x), own_sem.at[number]
        )

    def near_copy(number, way, q):
        return send_to(
            weights[number][0],
            part_of(number, core, q),
            near_send.at[number, way],
            near_recv.at[number, way],
            device(peers[(1, NX - 1)[way]], y, z, core),
        )

    def far_copy(number, way, q):
        place = part_of(number, core, q, way)
        return send_to(
            place,
            place,
            far_send.at[number, way],
            far_recv.at[number, way],
            device(peers[(1, NX - 1)[way]], y, z, core),
        )

    def part_copy(number, which, owner, src=None):
        place = part_of(number, owner, peers[which])
        return send_to(
            place if src is None else src,
            place,
            part_send.at[number, which],
            part_recv.at[number, which],
            partner,
        )

    def begin(copy):
        copy.start()
        sent.append(copy)

    def send_near(number):
        own_copy(number).start()
        for way in range(2):
            begin(near_copy(number, way, x))
        begin(part_copy(number, 0, core, weights[number][0]))

    def send_far(number):
        for way, q in ((0, peers[NX - 1]), (1, peers[1])):
            near_copy(number, way, q).wait_recv()
            begin(far_copy(number, way, q))
        begin(part_copy(number, 1, core))
        begin(part_copy(number, NX - 1, core))

    def share_far(number):
        for way in range(2):
            far_copy(number, way, peers[2]).wait_recv()
        begin(part_copy(number, 2, core))

    def settle(number):
        own_copy(number).wait()
        for which in range(NX):
            part_copy(number, which, 1 - core).wait_recv()

    send_near(0)
    send_near(1)

    row = lax.broadcasted_iota(jnp.int32, (PAGE, 128), 0)
    lane = lax.broadcasted_iota(jnp.int32, (PAGE, 128), 1)
    pages = CACHE // PAGE
    pool_page = lax.broadcasted_iota(jnp.int32, (pages, pages), 0)
    cache_page = lax.broadcasted_iota(jnp.int32, (pages, pages), 1)
    position = jnp.sum(
        jnp.where(table_ref[...] == pool_page, cache_page, 0).astype(F32),
        axis=1,
        keepdims=True,
    ).astype(jnp.int32)
    seen = length_ref[0] - position * PAGE
    for p in range(pages):
        hidden_row = (lane == 0) & (row >= seen[p : p + 1, :])
        keys[p * PAGE : (p + 1) * PAGE, 128:256] = jnp.where(
            hidden_row, MASKED_SCORE, 0.0
        ).astype(BF16)

    expert = lax.rem(row, 64)
    chosen = jnp.zeros((128, ROWS), F32)
    for k in range(routes_ref.shape[0]):
        chosen = chosen + jnp.where(
            routes_ref[k : k + 1, :] == expert, gates_ref[k : k + 1, :], 0.0
        )
    high_part = chosen.astype(BF16).astype(F32)
    route_rows[...] = jnp.where(row >= 64, chosen - high_part, high_part).T

    for j in range(1, NX):
        send_to(
            tokens_ref,
            tok.at[peers[NX - j]],
            tok_send.at[j],
            tok_recv.at[j],
            device(peers[j], y, z, core),
        ).wait_recv()
    whole = jnp.concatenate([tok[j].astype(F32) for j in range(NX)], axis=1)
    normed = norm_rows(whole, attn_gain_ref[...].reshape(1, WIDTH)).astype(BF16)
    for copy in loads:
        copy.wait()
    cosine = cos_ref[...]
    sine = sin_ref[...]
    scale = HEAD ** (-0.5)
    queries = jnp.dot(normed, qw[...], preferred_element_type=F32)
    first_bias = jnp.where(lane == 0, 1.0, 0.0).astype(BF16)
    for pair in range(HEADS // 2):
        block = queries[:, pair * 128 : (pair + 1) * 128]
        turned = (block * cosine + swap_halves(block) * sine).astype(BF16)
        turned = turned.astype(F32) * scale
        crossed = pltpu.roll(turned, HEAD, 1)
        for side in range(2):
            head = 2 * pair + side
            group = head // 3
            placed = turned if side == group else crossed
            mine = (lane < HEAD) if group == 0 else (lane >= HEAD)
            stacked[pl.ds(head * ROWS, ROWS), pl.ds(0, 128)] = jnp.where(
                mine, placed, 0.0
            ).astype(BF16)
            stacked[pl.ds(head * ROWS, ROWS), pl.ds(128, 128)] = first_bias
    new_keys = jnp.dot(normed, kw[...], preferred_element_type=F32)
    new_keys = (new_keys * cosine + swap_halves(new_keys) * sine).astype(BF16)
    new_values = jnp.dot(normed, vw[...], preferred_element_type=F32).astype(BF16)

    scores = lax.dot_general(
        stacked[:, 0:128],
        new_keys,
        (((1,), (1,)), ((), ())),
        preferred_element_type=F32,
    )
    query_row = lax.rem(lax.broadcasted_iota(jnp.int32, (STACK, ROWS), 0), ROWS)
    key_row = lax.broadcasted_iota(jnp.int32, (STACK, ROWS), 1)
    scores = jnp.where(key_row <= query_row, scores, MASKED_SCORE)
    top = jnp.max(scores, axis=1, keepdims=True)
    odds = jnp.exp(scores - top)
    best[...] = top
    total[...] = jnp.sum(odds, axis=1, keepdims=True)
    mix[...] = jnp.dot(odds.astype(BF16), new_values, preferred_element_type=F32)

    def step(i, carry):
        key_copy(i).wait()
        value_copy(i).wait()
        rows = pl.ds(pl.multiple_of(i * BLOCK, BLOCK), BLOCK)
        scores = lax.dot_general(
            stacked[...],
            keys[rows, :],
            (((1,), (1,)), ((), ())),
            preferred_element_type=F32,
        )
        old = best[...]
        new = jnp.maximum(old, jnp.max(scores, axis=1, keepdims=True))
        shrink = jnp.exp(old - new)
        odds = jnp.exp(scores - new)
        best[...] = new
        total[...] = total[...] * shrink + jnp.sum(odds, axis=1, keepdims=True)
        mix[...] = mix[...] * shrink + jnp.dot(
            odds.astype(BF16), values[rows, :], preferred_element_type=F32
        )
        return carry

    lax.fori_loop(0, 4, step, 0)
    send_far(0)
    send_near(2)
    lax.fori_loop(4, 7, step, 0)
    send_far(1)
    lax.fori_loop(7, BLOCKS, step, 0)
    result = mix[...] / total[...]
    pieces = []
    for pair in range(HEADS // 2):
        sides = []
        for side in range(2):
            head = 2 * pair + side
            block = result[head * ROWS : (head + 1) * ROWS, :]
            sides.append(block if side == head // 3 else pltpu.roll(block, HEAD, 1))
        pieces.append(jnp.where(lane < HEAD, sides[0], sides[1]).astype(BF16))
    attended = jnp.concatenate(pieces, axis=1)
    summand = jnp.dot(attended, ow[...], preferred_element_type=F32)
    for j in range(NX):
        quarter = summand[j * QUARTER : (j + 1) * QUARTER, :]
        partial[j] = quarter
        stage[j] = quarter.astype(BF16)
    for j in range(1, NX):
        copy = send_to(
            stage.at[peers[j]],
            arrived.at[x],
            sum_send.at[j],
            sum_recv.at[j],
            device(peers[j], y, z, core),
        )
        copy.start()
        sent.append(copy)

    my_rows = pl.ds(pl.multiple_of(x * QUARTER, QUARTER), QUARTER)
    residual = partial[x] + jnp.concatenate(
        [tok[j, my_rows, :].astype(F32) for j in range(NX)], axis=1
    )
    for j in range(1, NX):
        send_to(
            stage.at[peers[j]],
            arrived.at[peers[NX - j]],
            sum_send.at[j],
            sum_recv.at[j],
            device(peers[j], y, z, core),
        ).wait_recv()
        residual = residual + arrived[peers[NX - j]].astype(F32)
    residual = residual.astype(BF16)
    resid[...] = residual
    moe_in = norm_rows(residual.astype(F32), moe_gain_ref[...].reshape(1, WIDTH)).astype(BF16)
    augmented = jnp.concatenate([moe_in, route_rows[my_rows, :].astype(BF16)], axis=1)
    rows_a[z, y] = augmented[0:HALF]
    rows_b[y, z] = augmented[HALF:QUARTER]

    for j in (1, 3, 2):
        begin(
            send_to(
                rows_a.at[z, y],
                rows_a.at[z, y],
                ay_send.at[j],
                ay_recv.at[j],
                device(x, y_peers[j], z, core),
            )
        )
    to_z = lambda step: device(x, y, z_at(step), core)
    to_y = lambda step: device(x, y_peers[step % NY], z, core)
    near_y = (0, 1, 3, 2)
    near_z = (0, 1, -1, 2, -2, 3, -3, 4)
    gather_az = Gather(
        NZ, z, to_z, lambda i, s: rows_a.at[i, y_peers[near_y[s]]], NY, az_send, az_recv
    )
    gather_bz = Gather(NZ, z, to_z, lambda i, s: rows_b.at[y, i], 1, bz_send, bz_recv)
    gather_by = Gather(
        NY, y, to_y, lambda i, s: rows_b.at[i, z_at(near_z[s])], NZ, by_send, by_recv
    )
    gather_bz.send(0)
    gather_by.send(0, 0)
    gather_az.send(0, 0)

    def take_y(s):
        j = NY - near_y[s]
        place = rows_a.at[z, y_peers[near_y[s]]]
        send_to(
            place, place, ay_send.at[j], ay_recv.at[j], device(x, y_peers[j], z, core)
        ).wait_recv()
        gather_az.send(0, s)

    share_far(0)
    send_far(2)
    gather_bz.relay(0, 0)
    gather_by.send(0, 1)
    gather_by.send(0, 2)
    for s in range(1, NY):
        take_y(s)
    gather_az.relay(0, 0)
    gather_bz.relay(1, 0)
    gather_by.send(0, 3)
    gather_by.send(0, 4)
    gather_by.relay(0, 0)
    gather_az.relay(0, 1)
    gather_bz.relay(2, 0)
    gather_by.send(0, 5)
    gather_by.send(0, 6)
    gather_az.relay(0, 2, 3)
    gather_by.relay(0, 1, 2)
    gather_bz.wait(3)
    gather_by.send(0, 7)
    gather_az.relay(1, 0, 1)
    gather_by.relay(0, 3)
    gather_az.relay(1, 2, 3)
    gather_by.relay(0, 4)
    share_far(1)
    share_far(2)
    for number in range(3):
        settle(number)

    first_expert = 2 * (z * NY + y)

    def compute(rows, out, places):
        lead = rows.shape[1] * rows.shape[2]
        count = lead * len(places)
        block = jnp.concatenate([rows[i].reshape(lead, AUG) for i in places], axis=0)
        inputs = block[:, 0:WIDTH]
        gates = block[:, WIDTH:AUG].astype(F32)
        number = lax.rem(lax.broadcasted_iota(jnp.int32, (count, 128), 1), 64)
        answer = None
        for e in range(2):
            gate = jnp.sum(
                jnp.where(number == first_expert + e, gates, 0.0), axis=1, keepdims=True
            )
            gate_act = jnp.dot(inputs, wg[e], preferred_element_type=F32)
            up_act = jnp.dot(inputs, wu[e], preferred_element_type=F32)
            hidden = (gate_act / (1.0 + jnp.exp(-gate_act)) * up_act * gate).astype(BF16)
            term = jnp.dot(hidden, wd[e], preferred_element_type=F32)
            answer = term if answer is None else answer + term
        for at, i in enumerate(places):
            out[i] = answer[at * lead : (at + 1) * lead].reshape(
                rows.shape[1], rows.shape[2], WIDTH
            )

    far_y = (2, 1, 3, 0)
    far_z = (4, 3, -3, 2, -2, 1, -1, 0)
    scatter_az = Scatter(
        NZ,
        z,
        to_z,
        lambda i, s: out_a.at[i, y_peers[far_y[s]]],
        NY,
        stage_az,
        came_az,
        raz_send,
        raz_recv,
    )
    scatter_by = Scatter(
        NY,
        y,
        to_y,
        lambda i, s: out_b.at[i, z_at(far_z[s])],
        NZ,
        stage_by,
        came_by,
        rby_send,
        rby_recv,
    )
    scatter_bz = Scatter(
        NZ, z, to_z, lambda i, s: sum_b.at[i], 1, stage_bz, came_bz, rbz_send, rbz_recv
    )
    compute(rows_a, out_a, [z, z_at(1), z_at(-1), z_at(2)])
    gather_az.relay(2, 0, 1)
    gather_by.relay(0, 5, 6)
    gather_az.relay(2, 2, 3)
    gather_by.relay(0, 7)
    compute(rows_b, out_b, [y, y_peers[1]])
    for s in range(NY):
        gather_az.wait(3, s)
    compute(rows_a, out_a, [z_at(4), z_at(3), z_at(-3), z_at(-2)])
    for s in range(NY):
        scatter_az.send(0, s)
    for s in range(NZ):
        gather_by.wait(1, s)
    compute(rows_b, out_b, [y_peers[2], y_peers[3]])
    for s in range(NZ):
        scatter_by.send(0, s)
    for s in range(NY):
        scatter_az.send(1, s)
    for s in range(NZ):
        scatter_by.send(1, s)
        if s % 2:
            scatter_az.send(2, s // 2)

    def take_b(*parts):
        for s in parts:
            sum_b[z_at(far_z[s])] = scatter_by.result(s)

    def give_y(s):
        j = far_y[s]
        stage_ay[y_peers[j]] = scatter_az.result(s).astype(BF16)
        begin(
            send_to(
                stage_ay.at[y_peers[j]],
                came_ay.at[y],
                ry_send.at[j],
                ry_recv.at[j],
                device(x, y_peers[j], z, core),
            )
        )

    take_b(0)
    scatter_bz.send(0)
    scatter_az.send(3, 0)
    scatter_az.send(3, 1)
    take_b(1, 2)
    scatter_bz.send(1)
    scatter_az.send(3, 2)
    scatter_az.send(3, 3)
    take_b(3, 4)
    scatter_bz.send(2)
    give_y(0)
    take_b(5, 6)
    scatter_bz.send(3)
    give_y(1)
    give_y(2)
    upper = scatter_az.result(3)
    take_b(7)
    for j in range(1, NY):
        send_to(
            stage_ay.at[y_peers[j]],
            came_ay.at[y_peers[NY - j]],
            ry_send.at[j],
            ry_recv.at[j],
            device(x, y_peers[j], z, core),
        ).wait_recv()
        upper = upper + came_ay[y_peers[NY - j]].astype(F32)
    lower = scatter_bz.result()
    answer = resid[...].astype(F32) + jnp.concatenate([upper, lower], axis=0)
    answer = answer.astype(BF16)
    for j in range(NX):
        mixed[j] = answer[:, j * COLS : (j + 1) * COLS]
    for j in range(1, NX):
        copy = send_to(
            mixed.at[peers[j]],
            came_x.at[x],
            x_send.at[j],
            x_recv.at[j],
            device(peers[j], y, z, core),
        )
        copy.start()
        sent.append(copy)
    out_ref[pl.ds(pl.multiple_of(x * QUARTER, QUARTER), QUARTER), :] = mixed[x]
    for j in range(1, NX):
        source = peers[NX - j]
        send_to(
            mixed.at[peers[j]],
            came_x.at[source],
            x_send.at[j],
            x_recv.at[j],
            device(peers[j], y, z, core),
        ).wait_recv()
        out_ref[pl.ds(pl.multiple_of(source * QUARTER, QUARTER), QUARTER), :] = came_x[source]
    for copy in sent:
        copy.wait_send()
    for ring in (
        gather_az,
        gather_bz,
        gather_by,
        scatter_az,
        scatter_by,
        scatter_bz,
    ):
        for copy in ring.sent:
            copy.wait_send()


def shards(
    tokens,
    attn_gain,
    q_weight,
    key_matrix,
    value_matrix,
    o_weight,
    moe_gain,
    gate_weight,
    up_weight,
    down_weight,
    key_page_pool,
    value_page_pool,
    cache_lens,
    page_table,
    routes,
    route_gates,
):
    vmem = pl.BlockSpec(memory_space=pltpu.VMEM)
    smem = pl.BlockSpec(memory_space=pltpu.SMEM)
    hbm = pl.BlockSpec(memory_space=pl.ANY)
    dma = pltpu.SemaphoreType.DMA
    length = cache_lens[0]
    places = (length + jnp.arange(ROWS, dtype=jnp.int32)).astype(F32)
    entry = jnp.arange(128, dtype=jnp.int32) % HEAD
    frequency = 10000.0 ** (-2.0 * (entry % (HEAD // 2)).astype(F32) / HEAD)
    angle = places[:, None] * frequency
    cosine = jnp.cos(angle)
    sine = jnp.where(entry < HEAD // 2, -1.0, 1.0) * jnp.sin(angle)
    shape = jax.ShapeDtypeStruct
    pair = lambda *dims: pltpu.VMEM((2, *dims), BF16)
    both = lambda *dims: [dma(dims), dma(dims)]
    return pl.pallas_call(
        layer_kernel,
        out_shape=shape((ROWS, COLS), BF16),
        in_specs=[smem] + [vmem] * 8 + [hbm] * 9,
        out_specs=vmem,
        scratch_shapes=[
            pltpu.VMEM((NX, ROWS, COLS), BF16),
            pltpu.VMEM((WIDTH, COLS), BF16),
            pltpu.VMEM((WIDTH, 128), BF16),
            pltpu.VMEM((WIDTH, 128), BF16),
            pltpu.VMEM((COLS, WIDTH), BF16),
            pltpu.VMEM((CACHE, 256), BF16),
            pltpu.VMEM((CACHE, 128), BF16),
            pltpu.VMEM((STACK, 256), BF16),
            pltpu.VMEM((STACK, 1), F32),
            pltpu.VMEM((STACK, 1), F32),
            pltpu.VMEM((STACK, 128), F32),
            pltpu.VMEM((NX, QUARTER, WIDTH), BF16),
            pltpu.VMEM((NX, QUARTER, WIDTH), BF16),
            pltpu.VMEM((NX, QUARTER, WIDTH), F32),
            pltpu.VMEM((ROWS, 128), F32),
            pltpu.VMEM((QUARTER, WIDTH), BF16),
            pltpu.VMEM((NZ, NY, HALF, AUG), BF16),
            pltpu.VMEM((NY, NZ, HALF, AUG), BF16),
            pair(WIDTH, FFE),
            pair(WIDTH, FFE),
            pair(FFE, WIDTH),
            pltpu.VMEM((NZ, NY, HALF, WIDTH), F32),
            pltpu.VMEM((NY, NZ, HALF, WIDTH), F32),
            pltpu.VMEM((NZ, HALF, WIDTH), F32),
            pair(NZ // 2, NY, HALF, WIDTH),
            pair(NZ // 2, NY, HALF, WIDTH),
            pltpu.VMEM((NY, HALF, WIDTH), BF16),
            pltpu.VMEM((NY, HALF, WIDTH), BF16),
            pair(NY // 2, NZ, HALF, WIDTH),
            pair(NY // 2, NZ, HALF, WIDTH),
            pair(NZ // 2, 1, HALF, WIDTH),
            pair(NZ // 2, 1, HALF, WIDTH),
            pltpu.VMEM((NX, QUARTER, COLS), BF16),
            pltpu.VMEM((NX, QUARTER, COLS), BF16),
            dma((4,)),
            dma((BLOCKS,)),
            dma((BLOCKS,)),
            *both(NX),
            *both(NX),
            dma((3,)),
            *both(3, 2),
            *both(3, 2),
            *both(3, NX),
            *both(NY),
            *both(2, NZ // 2, NY),
            *both(2, NY // 2, NZ),
            *both(2, NZ // 2, 1),
            *both(NY),
            *both(2, NZ // 2, NY),
            *both(2, NY // 2, NZ),
            *both(2, NZ // 2, 1),
            *both(NX),
        ],
        compiler_params=pltpu.CompilerParams(
            collective_id=0, has_side_effects=True, vmem_limit_bytes=62 << 20
        ),
        name="layer",
    )(
        cache_lens,
        page_table,
        tokens,
        cosine,
        sine,
        routes.T,
        route_gates.T,
        attn_gain,
        moe_gain,
        q_weight,
        key_matrix,
        value_matrix,
        o_weight,
        key_page_pool.reshape(CACHE, 128),
        value_page_pool.reshape(CACHE, 128),
        gate_weight[0],
        up_weight[0],
        down_weight[0],
    )


def solution(mesh):
    in_specs = (
        P("seq", "tensor"),
        P(),
        P(None, "tensor"),
        P(None, "tensor"),
        P(None, "tensor"),
        P("tensor", None),
        P(),
        P("seq", None, "tensor"),
        P("seq", None, "tensor"),
        P("seq", "tensor", None),
        P("seq", None, "tensor"),
        P("seq", None, "tensor"),
        P("seq"),
        P("seq", None),
        P("seq", None),
        P("seq", None),
    )
    out_specs = P("seq", "tensor")
    return jax.shard_map(shards, mesh=mesh, in_specs=in_specs, out_specs=out_specs, check_vma=False)
```

```python
import jax
import jax.numpy as jnp
from jax import lax
from jax.experimental import pallas as pl
from jax.experimental.pallas import tpu as pltpu
from jax.sharding import PartitionSpec as P

MESH = pl.DeviceIdType.MESH
BF16 = jnp.bfloat16
F32 = jnp.float32
HEAD = 64
NORM_EPSILON = 1e-06
MASKED_SCORE = -1e30
NX, NY, NZ = 4, 4, 8
ROWS = 128
QUARTER = ROWS // NX
HALF = QUARTER // 2
WIDTH = 1536
COLS = WIDTH // NX
AUG = WIDTH + 128
HEADS = 6
STACK = HEADS * ROWS
CACHE = 8192
BLOCK = 1024
BLOCKS = CACHE // BLOCK
PAGE = 128
FFE = 512


def whereabouts():
    seq = lax.axis_index("seq")
    x = lax.axis_index("tensor")
    core = lax.rem(seq, 2)
    y = lax.rem(lax.div(seq, 2), NY)
    z = lax.div(seq, 2 * NY)
    return x, y, z, core


def device(x, y, z, core):
    return ((z * NY + y) * 2 + core, x)


def send_to(src, dst, send_sem, recv_sem, target):
    return pltpu.make_async_remote_copy(
        src_ref=src,
        dst_ref=dst,
        send_sem=send_sem,
        recv_sem=recv_sem,
        device_id=target,
        device_id_type=MESH,
    )


def greet(targets):
    barrier = pltpu.get_barrier_semaphore()
    for target in targets:
        pl.semaphore_signal(barrier, inc=1, device_id=target, device_id_type=MESH)
    pl.semaphore_wait(barrier, len(targets))


def norm_rows(widened, gain_row):
    return (
        widened
        * lax.rsqrt(jnp.mean(widened * widened, axis=1, keepdims=True) + NORM_EPSILON)
        * gain_row
    )


def swap_halves(block):
    lane = lax.broadcasted_iota(jnp.int32, block.shape, 1)
    return jnp.where(
        lax.rem(lane, HEAD) < HEAD // 2,
        pltpu.roll(block, 128 - HEAD // 2, 1),
        pltpu.roll(block, HEAD // 2, 1),
    )


class Gather:
    def __init__(self, size, me, target, place, parts, send_sem, recv_sem):
        self.size, self.me, self.target = size, me, target
        self.place, self.parts = place, parts
        self.send_sem, self.recv_sem = send_sem, recv_sem
        self.sent = []

    def copies(self, k, s, arriving):
        last = k + 1 == self.size // 2
        made = []
        for way in range(2):
            if last and self.parts > 1 and s // (self.parts // 2) != way:
                continue
            if arriving:
                shift = -(1 + k) if way == 0 else 1 + k
            else:
                shift = -k if way == 0 else k
            ref = self.place(lax.rem(self.me + shift + self.size, self.size), s)
            if last and self.parts == 1:
                ref = half_columns(ref)[way]
            made.append(
                send_to(
                    ref,
                    ref,
                    self.send_sem.at[way, k, s],
                    self.recv_sem.at[way, k, s],
                    self.target(1 if way == 0 else -1),
                )
            )
        return made

    def send(self, k, s=0):
        for copy in self.copies(k, s, False):
            copy.start()
            self.sent.append(copy)

    def wait(self, k, s=0):
        for copy in self.copies(k, s, True):
            copy.wait_recv()

    def relay(self, k, *parts):
        for s in parts:
            self.wait(k, s)
            self.send(k + 1, s)


class Scatter:
    def __init__(self, size, me, target, own, parts, stage, arrived, send_sem, recv_sem):
        self.size, self.me, self.target = size, me, target
        self.own, self.parts = own, parts
        self.stage, self.arrived = stage, arrived
        self.send_sem, self.recv_sem = send_sem, recv_sem
        self.sent = []

    def copy(self, way, k, s):
        src, dst = self.stage.at[way, k, s], self.arrived.at[way, k, s]
        if k == 0 and self.parts == 1:
            src, dst = half_columns(src)[way], half_columns(dst)[way]
        return send_to(
            src,
            dst,
            self.send_sem.at[way, k, s],
            self.recv_sem.at[way, k, s],
            self.target(1 if way == 0 else -1),
        )

    def send(self, k, s=0):
        distance = self.size // 2 - k
        for way in range(2):
            mine = self.parts == 1 or s // (self.parts // 2) == way
            if k == 0 and not mine:
                continue
            shift = distance if way == 0 else -distance
            own = self.own(lax.rem(self.me + shift + self.size, self.size), s)
            here = self.stage.at[way, k, s]
            if k == 0 and self.parts == 1:
                half_columns(here)[way][...] = half_columns(own)[way][...].astype(BF16)
            elif k == 0 or (k == 1 and not mine):
                here[...] = own[...].astype(BF16)
            elif k == 1 and self.parts == 1:
                self.copy(way, 0, s).wait_recv()
                came = half_columns(self.arrived.at[way, 0, s])[way]
                half_columns(here)[way][...] = (
                    half_columns(own)[way][...] + came[...].astype(F32)
                ).astype(BF16)
                half_columns(here)[1 - way][...] = half_columns(own)[1 - way][...].astype(BF16)
            else:
                self.copy(way, k - 1, s).wait_recv()
                here[...] = (own[...] + self.arrived[way, k - 1, s].astype(F32)).astype(BF16)
            copy = self.copy(way, k, s)
            copy.start()
            self.sent.append(copy)

    def result(self, s=0):
        k = self.size // 2 - 1
        answer = self.own(self.me, s)[...]
        for way in range(2):
            self.copy(way, k, s).wait_recv()
            answer = answer + self.arrived[way, k, s].astype(F32)
        return answer


def half_columns(ref):
    width = ref.shape[-1]
    split = (width // 256 + (width // 128) % 2) * 128
    lead = (slice(None),) * (len(ref.shape) - 1)
    return (
        ref.at[(*lead, pl.ds(0, split))],
        ref.at[(*lead, pl.ds(split, width - split))],
    )


def layer_kernel(
    length_ref,
    table_ref,
    tokens_ref,
    cos_ref,
    sin_ref,
    routes_ref,
    gates_ref,
    attn_gain_ref,
    moe_gain_ref,
    q_hbm,
    k_hbm,
    v_hbm,
    o_hbm,
    key_pool,
    value_pool,
    gate_hbm,
    up_hbm,
    down_hbm,
    out_ref,
    tok,
    qw,
    kw,
    vw,
    ow,
    keys,
    values,
    stacked,
    best,
    total,
    mix,
    stage,
    arrived,
    partial,
    route_rows,
    resid,
    rows_a,
    rows_b,
    wg,
    wu,
    wd,
    out_a,
    out_b,
    sum_b,
    stage_az,
    came_az,
    stage_ay,
    came_ay,
    stage_by,
    came_by,
    stage_bz,
    came_bz,
    mixed,
    came_x,
    load_sem,
    key_sem,
    value_sem,
    tok_send,
    tok_recv,
    sum_send,
    sum_recv,
    own_sem,
    near_send,
    near_recv,
    far_send,
    far_recv,
    part_send,
    part_recv,
    ay_send,
    ay_recv,
    az_send,
    az_recv,
    by_send,
    by_recv,
    bz_send,
    bz_recv,
    ry_send,
    ry_recv,
    raz_send,
    raz_recv,
    rby_send,
    rby_recv,
    rbz_send,
    rbz_recv,
    x_send,
    x_recv,
):
    x, y, z, core = whereabouts()
    peers = [lax.rem(x + j, NX) for j in range(NX)]
    y_peers = [lax.rem(y + j, NY) for j in range(NY)]
    z_at = lambda step: lax.rem(z + step + NZ, NZ)
    partner = device(x, y, z, 1 - core)
    sent = []
    loads = []
    for number, (src, dst) in enumerate(
        ((q_hbm, qw), (k_hbm, kw), (v_hbm, vw), (o_hbm, ow))
    ):
        copy = pltpu.make_async_copy(src, dst, load_sem.at[number])
        copy.start()
        loads.append(copy)

    def key_copy(i):
        rows = pl.ds(pl.multiple_of(i * BLOCK, BLOCK), BLOCK)
        return pltpu.make_async_copy(
            key_pool.at[rows, :], keys.at[rows, pl.ds(0, 128)], key_sem.at[i]
        )

    def value_copy(i):
        rows = pl.ds(pl.multiple_of(i * BLOCK, BLOCK), BLOCK)
        return pltpu.make_async_copy(
            value_pool.at[rows, :], values.at[rows, :], value_sem.at[i]
        )

    for i in range(BLOCKS):
        key_copy(i).start()
        value_copy(i).start()

    greet(
        [device(peers[j], y, z, core) for j in range(1, NX)]
        + [device(x, y_peers[j], z, core) for j in range(1, NY)]
        + [device(x, y, z_at(1), core), device(x, y, z_at(-1), core), partner]
    )
    for j in range(1, NX):
        copy = send_to(
            tokens_ref,
            tok.at[x],
            tok_send.at[j],
            tok_recv.at[j],
            device(peers[j], y, z, core),
        )
        copy.start()
        sent.append(copy)
    tok[x] = tokens_ref[...]

    weights = ((gate_hbm, wg), (up_hbm, wu), (down_hbm, wd))

    def part_of(number, owner, q, way=None):
        w = weights[number][1]
        size = (128 if number == 2 else WIDTH) // (1 if way is None else 2)
        first = 0 if way is None else way * size
        if number == 2:
            return w.at[owner, pl.ds(pl.multiple_of(q * 128 + first, 64), size), :]
        return w.at[owner, pl.ds(first, size), pl.ds(pl.multiple_of(q * 128, 128), 128)]

    def own_copy(number):
        return pltpu.make_async_copy(
            weights[number][0], part_of(number, core, x), own_sem.at[number]
        )

    def near_copy(number, way, q):
        return send_to(
            weights[number][0],
            part_of(number, core, q),
            near_send.at[number, way],
            near_recv.at[number, way],
            device(peers[(1, NX - 1)[way]], y, z, core),
        )

    def far_copy(number, way, q):
        place = part_of(number, core, q, way)
        return send_to(
            place,
            place,
            far_send.at[number, way],
            far_recv.at[number, way],
            device(peers[(1, NX - 1)[way]], y, z, core),
        )

    def part_copy(number, which, owner, src=None):
        place = part_of(number, owner, peers[which])
        return send_to(
            place if src is None else src,
            place,
            part_send.at[number, which],
            part_recv.at[number, which],
            partner,
        )

    def begin(copy):
        copy.start()
        sent.append(copy)

    def send_near(number):
        own_copy(number).start()
        for way in range(2):
            begin(near_copy(number, way, x))
        begin(part_copy(number, 0, core, weights[number][0]))

    def send_far(number):
        for way, q in ((0, peers[NX - 1]), (1, peers[1])):
            near_copy(number, way, q).wait_recv()
            begin(far_copy(number, way, q))
        begin(part_copy(number, 1, core))
        begin(part_copy(number, NX - 1, core))

    def share_far(number):
        for way in range(2):
            far_copy(number, way, peers[2]).wait_recv()
        begin(part_copy(number, 2, core))

    def settle(number):
        own_copy(number).wait()
        for which in range(NX):
            part_copy(number, which, 1 - core).wait_recv()

    send_near(0)
    send_near(1)

    row = lax.broadcasted_iota(jnp.int32, (PAGE, 128), 0)
    lane = lax.broadcasted_iota(jnp.int32, (PAGE, 128), 1)
    pages = CACHE // PAGE
    pool_page = lax.broadcasted_iota(jnp.int32, (pages, pages), 0)
    cache_page = lax.broadcasted_iota(jnp.int32, (pages, pages), 1)
    position = jnp.sum(
        jnp.where(table_ref[...] == pool_page, cache_page, 0).astype(F32),
        axis=1,
        keepdims=True,
    ).astype(jnp.int32)
    seen = length_ref[0] - position * PAGE
    for p in range(pages):
        hidden_row = (lane == 0) & (row >= seen[p : p + 1, :])
        keys[p * PAGE : (p + 1) * PAGE, 128:256] = jnp.where(
            hidden_row, MASKED_SCORE, 0.0
        ).astype(BF16)

    expert = lax.rem(row, 64)
    chosen = jnp.zeros((128, ROWS), F32)
    for k in range(routes_ref.shape[0]):
        chosen = chosen + jnp.where(
            routes_ref[k : k + 1, :] == expert, gates_ref[k : k + 1, :], 0.0
        )
    high_part = chosen.astype(BF16).astype(F32)
    route_rows[...] = jnp.where(row >= 64, chosen - high_part, high_part).T

    for j in range(1, NX):
        send_to(
            tokens_ref,
            tok.at[peers[NX - j]],
            tok_send.at[j],
            tok_recv.at[j],
            device(peers[j], y, z, core),
        ).wait_recv()
    whole = jnp.concatenate([tok[j].astype(F32) for j in range(NX)], axis=1)
    normed = norm_rows(whole, attn_gain_ref[...].reshape(1, WIDTH)).astype(BF16)
    for copy in loads:
        copy.wait()
    cosine = cos_ref[...]
    sine = sin_ref[...]
    scale = HEAD ** (-0.5)
    queries = jnp.dot(normed, qw[...], preferred_element_type=F32)
    first_bias = jnp.where(lane == 0, 1.0, 0.0).astype(BF16)
    for pair in range(HEADS // 2):
        block = queries[:, pair * 128 : (pair + 1) * 128]
        turned = (block * cosine + swap_halves(block) * sine).astype(BF16)
        turned = turned.astype(F32) * scale
        crossed = pltpu.roll(turned, HEAD, 1)
        for side in range(2):
            head = 2 * pair + side
            group = head // 3
            placed = turned if side == group else crossed
            mine = (lane < HEAD) if group == 0 else (lane >= HEAD)
            stacked[pl.ds(head * ROWS, ROWS), pl.ds(0, 128)] = jnp.where(
                mine, placed, 0.0
            ).astype(BF16)
            stacked[pl.ds(head * ROWS, ROWS), pl.ds(128, 128)] = first_bias
    new_keys = jnp.dot(normed, kw[...], preferred_element_type=F32)
    new_keys = (new_keys * cosine + swap_halves(new_keys) * sine).astype(BF16)
    new_values = jnp.dot(normed, vw[...], preferred_element_type=F32).astype(BF16)

    scores = lax.dot_general(
        stacked[:, 0:128],
        new_keys,
        (((1,), (1,)), ((), ())),
        preferred_element_type=F32,
    )
    query_row = lax.rem(lax.broadcasted_iota(jnp.int32, (STACK, ROWS), 0), ROWS)
    key_row = lax.broadcasted_iota(jnp.int32, (STACK, ROWS), 1)
    scores = jnp.where(key_row <= query_row, scores, MASKED_SCORE)
    top = jnp.max(scores, axis=1, keepdims=True)
    odds = jnp.exp(scores - top)
    best[...] = top
    total[...] = jnp.sum(odds, axis=1, keepdims=True)
    mix[...] = jnp.dot(odds.astype(BF16), new_values, preferred_element_type=F32)

    def step(i, carry):
        key_copy(i).wait()
        value_copy(i).wait()
        rows = pl.ds(pl.multiple_of(i * BLOCK, BLOCK), BLOCK)
        scores = lax.dot_general(
            stacked[...],
            keys[rows, :],
            (((1,), (1,)), ((), ())),
            preferred_element_type=F32,
        )
        old = best[...]
        new = jnp.maximum(old, jnp.max(scores, axis=1, keepdims=True))
        shrink = jnp.exp(old - new)
        odds = jnp.exp(scores - new)
        best[...] = new
        total[...] = total[...] * shrink + jnp.sum(odds, axis=1, keepdims=True)
        mix[...] = mix[...] * shrink + jnp.dot(
            odds.astype(BF16), values[rows, :], preferred_element_type=F32
        )
        return carry

    lax.fori_loop(0, 4, step, 0)
    send_far(0)
    lax.fori_loop(4, 7, step, 0)
    send_far(1)
    lax.fori_loop(7, BLOCKS, step, 0)
    result = mix[...] / total[...]
    pieces = []
    for pair in range(HEADS // 2):
        sides = []
        for side in range(2):
            head = 2 * pair + side
            block = result[head * ROWS : (head + 1) * ROWS, :]
            sides.append(block if side == head // 3 else pltpu.roll(block, HEAD, 1))
        pieces.append(jnp.where(lane < HEAD, sides[0], sides[1]).astype(BF16))
    attended = jnp.concatenate(pieces, axis=1)
    summand = jnp.dot(attended, ow[...], preferred_element_type=F32)
    for j in range(NX):
        quarter = summand[j * QUARTER : (j + 1) * QUARTER, :]
        partial[j] = quarter
        stage[j] = quarter.astype(BF16)
    for j in range(1, NX):
        copy = send_to(
            stage.at[peers[j]],
            arrived.at[x],
            sum_send.at[j],
            sum_recv.at[j],
            device(peers[j], y, z, core),
        )
        copy.start()
        sent.append(copy)

    send_near(2)

    my_rows = pl.ds(pl.multiple_of(x * QUARTER, QUARTER), QUARTER)
    residual = partial[x] + jnp.concatenate(
        [tok[j, my_rows, :].astype(F32) for j in range(NX)], axis=1
    )
    for j in range(1, NX):
        send_to(
            stage.at[peers[j]],
            arrived.at[peers[NX - j]],
            sum_send.at[j],
            sum_recv.at[j],
            device(peers[j], y, z, core),
        ).wait_recv()
        residual = residual + arrived[peers[NX - j]].astype(F32)
    residual = residual.astype(BF16)
    resid[...] = residual
    moe_in = norm_rows(residual.astype(F32), moe_gain_ref[...].reshape(1, WIDTH)).astype(BF16)
    augmented = jnp.concatenate([moe_in, route_rows[my_rows, :].astype(BF16)], axis=1)
    rows_a[z, y] = augmented[0:HALF]
    rows_b[y, z] = augmented[HALF:QUARTER]

    for j in (1, 3, 2):
        begin(
            send_to(
                rows_a.at[z, y],
                rows_a.at[z, y],
                ay_send.at[j],
                ay_recv.at[j],
                device(x, y_peers[j], z, core),
            )
        )
    to_z = lambda step: device(x, y, z_at(step), core)
    to_y = lambda step: device(x, y_peers[step % NY], z, core)
    near_y = (0, 1, 3, 2)
    near_z = (0, 1, -1, 2, -2, 3, -3, 4)
    gather_az = Gather(
        NZ, z, to_z, lambda i, s: rows_a.at[i, y_peers[near_y[s]]], NY, az_send, az_recv
    )
    gather_bz = Gather(NZ, z, to_z, lambda i, s: rows_b.at[y, i], 1, bz_send, bz_recv)
    gather_by = Gather(
        NY, y, to_y, lambda i, s: rows_b.at[i, z_at(near_z[s])], NZ, by_send, by_recv
    )
    gather_bz.send(0)
    gather_by.send(0, 0)
    gather_az.send(0, 0)

    def take_y(s):
        j = NY - near_y[s]
        place = rows_a.at[z, y_peers[near_y[s]]]
        send_to(
            place, place, ay_send.at[j], ay_recv.at[j], device(x, y_peers[j], z, core)
        ).wait_recv()
        gather_az.send(0, s)

    share_far(0)
    gather_bz.relay(0, 0)
    gather_by.send(0, 1)
    gather_by.send(0, 2)
    for s in range(1, NY):
        take_y(s)
    gather_az.relay(0, 0)
    gather_bz.relay(1, 0)
    gather_by.send(0, 3)
    gather_by.send(0, 4)
    gather_by.relay(0, 0)
    gather_az.relay(0, 1)
    gather_bz.relay(2, 0)
    gather_by.send(0, 5)
    gather_by.send(0, 6)
    gather_az.relay(0, 2, 3)
    send_far(2)
    gather_by.relay(0, 1, 2)
    gather_bz.wait(3)
    gather_by.send(0, 7)
    gather_az.relay(1, 0, 1)
    gather_by.relay(0, 3)
    gather_az.relay(1, 2, 3)
    gather_by.relay(0, 4)
    share_far(1)
    share_far(2)
    for number in range(3):
        settle(number)

    first_expert = 2 * (z * NY + y)

    def compute(rows, out, places):
        lead = rows.shape[1] * rows.shape[2]
        count = lead * len(places)
        block = jnp.concatenate([rows[i].reshape(lead, AUG) for i in places], axis=0)
        inputs = block[:, 0:WIDTH]
        gates = block[:, WIDTH:AUG].astype(F32)
        number = lax.rem(lax.broadcasted_iota(jnp.int32, (count, 128), 1), 64)
        answer = None
        for e in range(2):
            gate = jnp.sum(
                jnp.where(number == first_expert + e, gates, 0.0), axis=1, keepdims=True
            )
            gate_act = jnp.dot(inputs, wg[e], preferred_element_type=F32)
            up_act = jnp.dot(inputs, wu[e], preferred_element_type=F32)
            hidden = (gate_act / (1.0 + jnp.exp(-gate_act)) * up_act * gate).astype(BF16)
            term = jnp.dot(hidden, wd[e], preferred_element_type=F32)
            answer = term if answer is None else answer + term
        for at, i in enumerate(places):
            out[i] = answer[at * lead : (at + 1) * lead].reshape(
                rows.shape[1], rows.shape[2], WIDTH
            )

    far_y = (2, 1, 3, 0)
    far_z = (4, 3, -3, 2, -2, 1, -1, 0)
    scatter_az = Scatter(
        NZ,
        z,
        to_z,
        lambda i, s: out_a.at[i, y_peers[far_y[s]]],
        NY,
        stage_az,
        came_az,
        raz_send,
        raz_recv,
    )
    scatter_by = Scatter(
        NY,
        y,
        to_y,
        lambda i, s: out_b.at[i, z_at(far_z[s])],
        NZ,
        stage_by,
        came_by,
        rby_send,
        rby_recv,
    )
    scatter_bz = Scatter(
        NZ, z, to_z, lambda i, s: sum_b.at[i], 1, stage_bz, came_bz, rbz_send, rbz_recv
    )
    compute(rows_a, out_a, [z, z_at(1), z_at(-1), z_at(2)])
    gather_az.relay(2, 0, 1)
    gather_by.relay(0, 5, 6)
    gather_az.relay(2, 2, 3)
    gather_by.relay(0, 7)
    compute(rows_b, out_b, [y, y_peers[1]])
    for s in range(NY):
        gather_az.wait(3, s)
    compute(rows_a, out_a, [z_at(4), z_at(3), z_at(-3), z_at(-2)])
    for s in range(NY):
        scatter_az.send(0, s)
    for s in range(NZ):
        gather_by.wait(1, s)
    compute(rows_b, out_b, [y_peers[2], y_peers[3]])
    for s in range(NZ):
        scatter_by.send(0, s)
    for s in range(NY):
        scatter_az.send(1, s)
    for s in range(NZ):
        scatter_by.send(1, s)
        if s % 2:
            scatter_az.send(2, s // 2)

    def take_b(*parts):
        for s in parts:
            sum_b[z_at(far_z[s])] = scatter_by.result(s)

    def give_y(s):
        j = far_y[s]
        stage_ay[y_peers[j]] = scatter_az.result(s).astype(BF16)
        begin(
            send_to(
                stage_ay.at[y_peers[j]],
                came_ay.at[y],
                ry_send.at[j],
                ry_recv.at[j],
                device(x, y_peers[j], z, core),
            )
        )

    take_b(0)
    scatter_bz.send(0)
    scatter_az.send(3, 0)
    scatter_az.send(3, 1)
    take_b(1, 2)
    scatter_bz.send(1)
    scatter_az.send(3, 2)
    scatter_az.send(3, 3)
    take_b(3, 4)
    scatter_bz.send(2)
    give_y(0)
    take_b(5, 6)
    scatter_bz.send(3)
    give_y(1)
    give_y(2)
    upper = scatter_az.result(3)
    take_b(7)
    for j in range(1, NY):
        send_to(
            stage_ay.at[y_peers[j]],
            came_ay.at[y_peers[NY - j]],
            ry_send.at[j],
            ry_recv.at[j],
            device(x, y_peers[j], z, core),
        ).wait_recv()
        upper = upper + came_ay[y_peers[NY - j]].astype(F32)
    lower = scatter_bz.result()
    answer = resid[...].astype(F32) + jnp.concatenate([upper, lower], axis=0)
    answer = answer.astype(BF16)
    for j in range(NX):
        mixed[j] = answer[:, j * COLS : (j + 1) * COLS]
    for j in range(1, NX):
        copy = send_to(
            mixed.at[peers[j]],
            came_x.at[x],
            x_send.at[j],
            x_recv.at[j],
            device(peers[j], y, z, core),
        )
        copy.start()
        sent.append(copy)
    out_ref[pl.ds(pl.multiple_of(x * QUARTER, QUARTER), QUARTER), :] = mixed[x]
    for j in range(1, NX):
        source = peers[NX - j]
        send_to(
            mixed.at[peers[j]],
            came_x.at[source],
            x_send.at[j],
            x_recv.at[j],
            device(peers[j], y, z, core),
        ).wait_recv()
        out_ref[pl.ds(pl.multiple_of(source * QUARTER, QUARTER), QUARTER), :] = came_x[source]
    for copy in sent:
        copy.wait_send()
    for ring in (
        gather_az,
        gather_bz,
        gather_by,
        scatter_az,
        scatter_by,
        scatter_bz,
    ):
        for copy in ring.sent:
            copy.wait_send()


def shards(
    tokens,
    attn_gain,
    q_weight,
    key_matrix,
    value_matrix,
    o_weight,
    moe_gain,
    gate_weight,
    up_weight,
    down_weight,
    key_page_pool,
    value_page_pool,
    cache_lens,
    page_table,
    routes,
    route_gates,
):
    vmem = pl.BlockSpec(memory_space=pltpu.VMEM)
    smem = pl.BlockSpec(memory_space=pltpu.SMEM)
    hbm = pl.BlockSpec(memory_space=pl.ANY)
    dma = pltpu.SemaphoreType.DMA
    length = cache_lens[0]
    places = (length + jnp.arange(ROWS, dtype=jnp.int32)).astype(F32)
    entry = jnp.arange(128, dtype=jnp.int32) % HEAD
    frequency = 10000.0 ** (-2.0 * (entry % (HEAD // 2)).astype(F32) / HEAD)
    angle = places[:, None] * frequency
    cosine = jnp.cos(angle)
    sine = jnp.where(entry < HEAD // 2, -1.0, 1.0) * jnp.sin(angle)
    shape = jax.ShapeDtypeStruct
    pair = lambda *dims: pltpu.VMEM((2, *dims), BF16)
    both = lambda *dims: [dma(dims), dma(dims)]
    return pl.pallas_call(
        layer_kernel,
        out_shape=shape((ROWS, COLS), BF16),
        in_specs=[smem] + [vmem] * 8 + [hbm] * 9,
        out_specs=vmem,
        scratch_shapes=[
            pltpu.VMEM((NX, ROWS, COLS), BF16),
            pltpu.VMEM((WIDTH, COLS), BF16),
            pltpu.VMEM((WIDTH, 128), BF16),
            pltpu.VMEM((WIDTH, 128), BF16),
            pltpu.VMEM((COLS, WIDTH), BF16),
            pltpu.VMEM((CACHE, 256), BF16),
            pltpu.VMEM((CACHE, 128), BF16),
            pltpu.VMEM((STACK, 256), BF16),
            pltpu.VMEM((STACK, 1), F32),
            pltpu.VMEM((STACK, 1), F32),
            pltpu.VMEM((STACK, 128), F32),
            pltpu.VMEM((NX, QUARTER, WIDTH), BF16),
            pltpu.VMEM((NX, QUARTER, WIDTH), BF16),
            pltpu.VMEM((NX, QUARTER, WIDTH), F32),
            pltpu.VMEM((ROWS, 128), F32),
            pltpu.VMEM((QUARTER, WIDTH), BF16),
            pltpu.VMEM((NZ, NY, HALF, AUG), BF16),
            pltpu.VMEM((NY, NZ, HALF, AUG), BF16),
            pair(WIDTH, FFE),
            pair(WIDTH, FFE),
            pair(FFE, WIDTH),
            pltpu.VMEM((NZ, NY, HALF, WIDTH), F32),
            pltpu.VMEM((NY, NZ, HALF, WIDTH), F32),
            pltpu.VMEM((NZ, HALF, WIDTH), F32),
            pair(NZ // 2, NY, HALF, WIDTH),
            pair(NZ // 2, NY, HALF, WIDTH),
            pltpu.VMEM((NY, HALF, WIDTH), BF16),
            pltpu.VMEM((NY, HALF, WIDTH), BF16),
            pair(NY // 2, NZ, HALF, WIDTH),
            pair(NY // 2, NZ, HALF, WIDTH),
            pair(NZ // 2, 1, HALF, WIDTH),
            pair(NZ // 2, 1, HALF, WIDTH),
            pltpu.VMEM((NX, QUARTER, COLS), BF16),
            pltpu.VMEM((NX, QUARTER, COLS), BF16),
            dma((4,)),
            dma((BLOCKS,)),
            dma((BLOCKS,)),
            *both(NX),
            *both(NX),
            dma((3,)),
            *both(3, 2),
            *both(3, 2),
            *both(3, NX),
            *both(NY),
            *both(2, NZ // 2, NY),
            *both(2, NY // 2, NZ),
            *both(2, NZ // 2, 1),
            *both(NY),
            *both(2, NZ // 2, NY),
            *both(2, NY // 2, NZ),
            *both(2, NZ // 2, 1),
            *both(NX),
        ],
        compiler_params=pltpu.CompilerParams(
            collective_id=0, has_side_effects=True, vmem_limit_bytes=62 << 20
        ),
        name="layer",
    )(
        cache_lens,
        page_table,
        tokens,
        cosine,
        sine,
        routes.T,
        route_gates.T,
        attn_gain,
        moe_gain,
        q_weight,
        key_matrix,
        value_matrix,
        o_weight,
        key_page_pool.reshape(CACHE, 128),
        value_page_pool.reshape(CACHE, 128),
        gate_weight[0],
        up_weight[0],
        down_weight[0],
    )


def solution(mesh):
    in_specs = (
        P("seq", "tensor"),
        P(),
        P(None, "tensor"),
        P(None, "tensor"),
        P(None, "tensor"),
        P("tensor", None),
        P(),
        P("seq", None, "tensor"),
        P("seq", None, "tensor"),
        P("seq", "tensor", None),
        P("seq", None, "tensor"),
        P("seq", None, "tensor"),
        P("seq"),
        P("seq", None),
        P("seq", None),
        P("seq", None),
    )
    out_specs = P("seq", "tensor")
    return jax.shard_map(shards, mesh=mesh, in_specs=in_specs, out_specs=out_specs, check_vma=False)
```
